256 devices in a mesh: space: 32 (over x, z), chan: 8 (over y, core).
Axes of the slice: x: 4, y: 4, z: 8, core: 2. Of those that a mesh axis runs over, the one named last changes fastest.
Arguments:
- hidden: bfloat16 [96, 147456], P('space', 'chan'), may hold values from -3 to 3
- conditioning: bfloat16 [2, 96, 36864], P(None, 'space', 'chan'), may hold values from -6 to 6
- gate_weight: bfloat16 [1920, 27648], P('space', 'chan'), may hold values from -0.046875 to 0.046875
- gate_bias: float32 [2, 1536], P(None, 'chan'), may hold values from -4 to 4
- cand_weight: bfloat16 [960, 27648], P('space', 'chan'), may hold values from -0.046875 to 0.046875
- cand_bias: float32 [1536], P('chan'), may hold values from -4 to 4
Outputs:
- states: bfloat16 [2, 96, 147456], P(None, 'space', 'chan')
The draws below stay inside these ranges and needn't reach their ends.
All inputs are finite; a program needn't handle non-finite values.
Results may differ from the reference program's by a relative error of at most 0.0026.
Values may be sent and summed in bfloat16 or wider, within the bound.
A program may use at most 192 MiB of HBM per device.

```python
import jax
import jax.numpy as jnp

C = 1536
CC = 384
H = 96
W = 96
STEPS = 2
CIN = 1920


def level_of(own_key, dims, shards, least, largest):
    def one(dim, parts):
        steps = jax.random.uniform(jax.random.fold_in(jax.random.fold_in(own_key, 6), dim), (parts,), jnp.float32, least / len(shards), largest / len(shards))
        return jnp.repeat(jnp.exp(steps), dims[dim] // parts).reshape((-1,) + (1,) * (len(dims) - dim - 1))

    gain = one(*shards[0])
    for cut in shards[1:]:
        gain = gain * one(*cut)
    return gain


def noise(stream_key, shape, spread, bound, pieces=(), kind=jnp.bfloat16):
    level = level_of(stream_key, shape, pieces, -0.22, 0.18) if pieces else 1.0
    entries = jax.random.normal(stream_key, shape, jnp.float32) * spread * level
    return jnp.minimum(jnp.maximum(entries, -bound), bound).astype(kind)


def setup_inputs(seed: int = 0) -> dict:
    splits = jax.random.split(jax.random.key(seed), 7)
    hidden = noise(splits[0], (H, C * W), 0.5, 3.0, ((0, 32), (1, 8)))
    conditioning = noise(splits[1], (STEPS, H, CC * W), 1.0, 6.0, ((1, 32), (2, 8)))
    gate_weight = noise(splits[2], (CIN, C * 18), (9 * CIN) ** -0.5, 0.046875, ((0, 32), (1, 8)))
    gate_bias = noise(splits[3], (2, C), 1.0, 4.0, ((1, 8),), jnp.float32)
    cand_weight = noise(splits[4], (CIN // 2, C * 18), (9 * CIN) ** -0.5, 0.046875, ((0, 32), (1, 8)))
    cand_bias = noise(splits[5], (C,), 1.0, 4.0, ((0, 8),), jnp.float32)
    return dict(hidden=hidden, conditioning=conditioning, gate_weight=gate_weight, gate_bias=gate_bias, cand_weight=cand_weight, cand_bias=cand_bias)


def convolve(padded, kernel):
    row_count = padded.shape[0] - 2
    col_count = padded.shape[1] - 2
    channels = padded.shape[2]
    running = jnp.zeros((row_count * col_count, kernel.shape[3]), jnp.float32)
    for tap_row in range(3):
        for tap_col in range(3):
            window = padded[tap_row:tap_row + row_count, tap_col:tap_col + col_count, :].reshape(row_count * col_count, channels)
            running = running + jnp.dot(window, kernel[tap_row, tap_col], preferred_element_type=jnp.float32)
    return running


def pad_grid(field):
    return jnp.pad(field, ((1, 1), (1, 1), (0, 0)))


def reference(hidden, conditioning, gate_weight, gate_bias, cand_weight, cand_bias):
    state = hidden.reshape(H, C, W).transpose(0, 2, 1)
    cond_grid = conditioning.reshape(STEPS, H, CC, W).transpose(0, 1, 3, 2)
    gate_kernel = gate_weight.reshape(CIN, C, 2, 3, 3).transpose(3, 4, 0, 2, 1).reshape(3, 3, CIN, 2 * C)
    cand_kernel = cand_weight.reshape(CIN // 2, C, 2, 3, 3).transpose(3, 4, 0, 2, 1).reshape(3, 3, CIN, C)
    frames = []
    for moment in range(STEPS):
        joined = jnp.concatenate([cond_grid[moment], state], axis=2)
        preact = convolve(pad_grid(joined), gate_kernel) + gate_bias.reshape(2 * C)
        update = jax.nn.sigmoid(preact[:, :C])
        reset = jax.nn.sigmoid(preact[:, C:])
        previous = state.astype(jnp.float32).reshape(H * W, C)
        gated = (reset * previous).astype(jnp.bfloat16).reshape(H, W, C)
        cand_input = jnp.concatenate([cond_grid[moment], gated], axis=2)
        candidate = jnp.tanh(convolve(pad_grid(cand_input), cand_kernel) + cand_bias)
        state = ((1.0 - update) * previous + update * candidate).astype(jnp.bfloat16).reshape(H, W, C)
        frames.append(state.transpose(0, 2, 1).reshape(H, C * W))
    return jnp.stack(frames)
```

```python
import functools

import jax
import jax.numpy as jnp
from jax import lax
from jax.experimental import pallas as pl
from jax.experimental.pallas import tpu as pltpu
from jax.sharding import PartitionSpec as P

W = 96
ROWS = 3
CELLS = ROWS * W
HALO = (ROWS + 2) * W
OWN = 192
COND = 48
SHARD = 60
SLOT = 64
WIN = 256
BF = jnp.bfloat16
F32 = jnp.float32
PAIRS = tuple(
    (t, n)
    for t in range(1, 8)
    for n in range(8)
    if max(240 * t, 384 + 192 * n) < min(240 * t + 240, 576 + 192 * n)
)


def gate_taps(raw):
    taps = raw.reshape(30, 2, OWN, 2, 9).transpose(4, 1, 0, 3, 2)
    taps = jnp.pad(taps, ((0, 0), (0, 0), (0, 2), (0, 0), (0, 0)))
    return taps.reshape(9, SLOT, 2 * OWN)


def cand_taps(raw):
    taps = raw.reshape(30, OWN, 2, 9).transpose(3, 2, 0, 1)
    taps = jnp.pad(taps, ((0, 0), (0, 0), (0, 2), (0, 0)))
    return taps.reshape(9, SLOT, OWN)


def kernel(
    act_ref, wg_ref, wc_ref, bias_ref, out_ref,
    init, gbuf0, sbuf, gbuf1, wg, wc, xs, emat, acc, cacc, upd, prev,
    gated, fresh, landed, sib_bias,
    xsend, xrecv, wsend, wz, wl, wr, wo, wd, osem, orecv, bsem,
):
    s = lax.axis_index("space")
    ch = lax.axis_index("chan")
    x, z = s // 8, s % 8
    b, y, c = z % 2, ch // 2, ch % 2
    job_row = s - b + c
    job_chan = 2 * y + b
    right = (x + 1) % 4
    left = (x + 3) % 4
    opposite = (x + 2) % 4

    barrier = pltpu.get_barrier_semaphore()

    def greet(space, chan):
        pl.semaphore_signal(
            barrier, inc=1, device_id=(space, chan), device_id_type=pl.DeviceIdType.MESH
        )

    def greet_line(i, carry):
        space, chan = 8 * x + i // 8, i % 8

        @pl.when(jnp.logical_or(space != s, chan != ch))
        def _():
            greet(space, chan)

        return carry

    lax.fori_loop(0, 64, greet_line, 0)
    greet(8 * right + z, ch)
    greet(8 * left + z, ch)

    @pl.when(z < 2)
    def _():
        lax.fori_loop(0, 16, lambda i, k: (greet(8 * left + 6 + i // 8, i % 8), k)[1], 0)

    @pl.when(z >= 6)
    def _():
        lax.fori_loop(0, 16, lambda i, k: (greet(8 * right + i // 8, i % 8), k)[1], 0)

    at_end = jnp.logical_or(z < 2, z >= 6)
    pl.semaphore_wait(barrier, 65 + 16 * at_end.astype(jnp.int32))

    def remote(src, dst, send, recv, space, chan):
        return pltpu.make_async_remote_copy(
            src_ref=src, dst_ref=dst, send_sem=send, recv_sem=recv,
            device_id=(space, chan), device_id_type=pl.DeviceIdType.MESH,
        )

    def push(src, dst, send, recv, space, chan):
        mine = jnp.logical_and(space == s, chan == ch)

        @pl.when(mine)
        def _():
            pltpu.make_async_copy(src, dst, recv).start()

        @pl.when(jnp.logical_not(mine))
        def _():
            remote(src, dst, send, recv, space, chan).start()

    def sent(src, dst, send, recv, space, chan):
        mine = jnp.logical_and(space == s, chan == ch)

        @pl.when(jnp.logical_not(mine))
        def _():
            remote(src, dst, send, recv, space, chan).wait_send()

    def arrived(dst, recv):
        pltpu.make_async_copy(dst, dst, recv).wait()

    def exchange(act, k, row, chan, src, buf):
        def one(i, carry):
            kind, p = i // 8, i % 8
            to_row = (row + jnp.where(kind == 0, 0, jnp.where(kind == 1, 1, 31))) % 32
            space = to_row - to_row % 2 + p % 2
            dest = p - p % 2 + to_row % 2

            @pl.when(kind == 0)
            def _():
                act(src, buf.at[chan, pl.ds(W, CELLS)], xsend.at[i], xrecv.at[k, 0, chan], space, dest)

            @pl.when(kind == 1)
            def _():
                act(src.at[pl.ds(2 * W, W)], buf.at[chan, pl.ds(0, W)], xsend.at[i],
                    xrecv.at[k, 1, chan], space, dest)

            @pl.when(kind == 2)
            def _():
                act(src.at[pl.ds(0, W)], buf.at[chan, pl.ds(4 * W, W)], xsend.at[i],
                    xrecv.at[k, 2, chan], space, dest)

            return carry

        lax.fori_loop(0, 24, one, 0)

    def exchanged(k, buf):
        def one(n, carry):
            arrived(buf.at[n, pl.ds(W, CELLS)], xrecv.at[k, 0, n])
            arrived(buf.at[n, pl.ds(0, W)], xrecv.at[k, 1, n])
            arrived(buf.at[n, pl.ds(4 * W, W)], xrecv.at[k, 2, n])
            return carry

        lax.fori_loop(0, 8, one, 0)

    group = z // 4
    spot = z % 4
    mine = ((wg_ref, wg), (wc_ref, wc))

    def kernel_z(kind, act):
        src, buf = mine[kind]

        def one(i, carry):
            act(src, buf.at[2 * x + group, :, spot], wsend.at[kind, i], wz.at[kind, spot],
                8 * x + 2 * i + c, 2 * y + group)
            return carry

        lax.fori_loop(0, 4, one, 0)

    here, lower, upper, across = 2 * x + c, 2 * left + c, 2 * right + c, 2 * opposite + c

    def hop(kind, t, i, send, recv, space, chan):
        buf = mine[kind][1]
        return remote(buf.at[t, :, i], buf.at[t, :, i], wsend.at[kind, send], recv, space, chan)

    def go_right(kind, i):
        return hop(kind, here, i, 4 + i, wl.at[kind, i], 8 * right + z, ch)

    def go_left(kind, i):
        return hop(kind, here, i, 8 + i, wr.at[kind, i], 8 * left + z, ch)

    def pass_right(kind, i):
        return hop(kind, lower, i, 12 + i, wo.at[kind, i], 8 * right + z, ch)

    def pass_left(kind, i):
        return hop(kind, upper, i, 12 + i, wo.at[kind, i], 8 * left + z, ch)

    def share(kind, j, i):
        t = (here, lower, upper, across)[j]
        return hop(kind, t, i, 16 + 4 * j + i, wd.at[kind, j, i], s, 2 * y + 1 - c)

    def piece(kind, t, i):
        return mine[kind][1].at[t, :, i]

    def kernel_own(kind):
        for i in range(4):
            arrived(piece(kind, here, i), wz.at[kind, i])
            go_right(kind, i).start()
            go_left(kind, i).start()
            share(kind, 0, i).start()

    def kernel_sides(kind):
        for i in range(4):
            arrived(piece(kind, lower, i), wl.at[kind, i])
            if i % 2 == 0:
                pass_right(kind, i).start()
            share(kind, 1, i).start()
            arrived(piece(kind, upper, i), wr.at[kind, i])
            if i % 2 == 1:
                pass_left(kind, i).start()
            share(kind, 2, i).start()

    def kernel_across(kind):
        for i in range(4):
            arrived(piece(kind, across, i), wo.at[kind, i])
            share(kind, 3, i).start()

    def kernel_shared(kind, j):
        t = 2 * ((here, lower, upper, across)[j] // 2) + 1 - c
        for i in range(4):
            arrived(piece(kind, t, i), wd.at[kind, j, i])
        return t

    def kernel_sent(kind):
        kernel_z(kind, sent)
        for i in range(4):
            go_right(kind, i).wait_send()
            go_left(kind, i).wait_send()
            if i % 2 == 0:
                pass_right(kind, i).wait_send()
            else:
                pass_left(kind, i).wait_send()
            for j in range(4):
                share(kind, j, i).wait_send()

    def slot_channel(t, rows):
        j = lax.broadcasted_iota(jnp.int32, (rows, WIN), 1)
        r = j % SLOT
        m = r % 32
        k = SHARD * (4 * t + j // SLOT) + 2 * m + r // 32
        return jnp.where(m < 30, k, -1)

    def spread(t, v):
        cell = lax.broadcasted_iota(jnp.int32, (HALO, WIN), 0)
        col = cell % W
        inside = jnp.logical_and(
            jnp.logical_or(cell >= W, job_row > 0),
            jnp.logical_or(cell < 4 * W, job_row < 31),
        )
        v = jnp.where(inside, v, 0.0)
        low = jnp.where(col == 0, 0.0, pltpu.roll(v, 1, 0))
        high = jnp.where(col == W - 1, 0.0, pltpu.roll(v, HALO - 1, 0))
        xs[:, 768 * t:768 * t + 256] = low.astype(BF)
        xs[:, 768 * t + 256:768 * t + 512] = v.astype(BF)
        xs[:, 768 * t + 512:768 * t + 768] = high.astype(BF)

    def cond_slots(step, t):
        v = jnp.zeros((HALO, WIN), F32)
        lane = lax.broadcasted_iota(jnp.int32, (128, WIN), 0)
        want = slot_channel(t, 128)
        for n in range(5 * t, min(8, 5 * t + 5)):
            here_n = jnp.logical_and(lane >= COND * step, lane < COND * step + COND)
            hit = jnp.logical_and(here_n, want == COND * n + lane - COND * step)
            e = hit.astype(F32).astype(BF)
            v = v + jnp.dot(init[n, :, 0:128], e, preferred_element_type=F32)
        return v

    def build(step, buf, base, first):
        if first:
            spread(0, cond_slots(step, 0))
        for t in range(1, 8):
            v = cond_slots(step, 1) if t == 1 else jnp.zeros((HALO, WIN), F32)
            for q, (pt, n) in enumerate(PAIRS):
                if pt == t:
                    v = v + jnp.dot(buf[n, :, base:base + OWN], emat[q], preferred_element_type=F32)
            spread(t, v)

    def window(buf, total, t):
        lane = pl.multiple_of(768 * t, 768)
        out = total.shape[1]
        for a in range(3):
            total[...] += jnp.dot(
                xs[pl.ds(a * W, CELLS), pl.ds(lane, 768)],
                buf[t, 3 * a:3 * a + 3].reshape(768, out),
                preferred_element_type=F32,
            )

    def bias(row):
        return jnp.where(b == c, bias_ref[row:row + 1, 0:OWN], sib_bias[row:row + 1, 0:OWN])

    def finish_gate(k):
        pre = acc[...]
        upd[...] = jax.nn.sigmoid(pre[:, :OWN] + bias(0))
        reset = jax.nn.sigmoid(pltpu.roll(pre, OWN, 1)[:, :OWN] + bias(1))
        gated[k] = (reset * prev[...]).astype(BF)

    def finish_cand(k):
        candidate = jnp.tanh(cacc[...] + bias(2))
        u = upd[...]
        new = ((1.0 - u) * prev[...] + u * candidate).astype(BF)
        fresh[k] = new
        prev[...] = new.astype(F32)

    def deliver(k, act):
        act(fresh.at[k], landed.at[k], osem.at[k], orecv.at[k], job_row, job_chan)

    exchange(push, 0, s, ch, act_ref, init)
    bias_copy = remote(bias_ref, sib_bias, bsem.at[0], bsem.at[1], s, 2 * y + 1 - c)
    bias_copy.start()
    kernel_z(0, push)
    kernel_z(1, push)
    for q, (t, n) in enumerate(PAIRS):
        lane = lax.broadcasted_iota(jnp.int32, (OWN, WIN), 0)
        hit = slot_channel(t, OWN) == 384 + 192 * n + lane
        emat[q] = hit.astype(F32).astype(BF)
    acc[...] = jnp.zeros_like(acc)
    cacc[...] = jnp.zeros_like(cacc)
    kernel_own(0)
    exchanged(0, init)
    exchange(sent, 0, s, ch, act_ref, init)
    bias_copy.wait()
    prev[...] = init[job_chan, pl.ds(W, CELLS), 128:128 + OWN].astype(F32)
    build(0, init, 128, True)

    window(wg, acc, here)
    kernel_sides(0)
    kernel_own(1)

    def shared_window(kind, buf, total, j):
        window(buf, total, kernel_shared(kind, j))

    window(wg, acc, lower)
    window(wg, acc, upper)
    shared_window(0, wg, acc, 0)
    shared_window(0, wg, acc, 1)
    shared_window(0, wg, acc, 2)
    kernel_across(0)
    window(wg, acc, across)
    shared_window(0, wg, acc, 3)
    finish_gate(0)
    exchange(push, 1, job_row, job_chan, gated.at[0], gbuf0)
    kernel_sides(1)
    exchanged(1, gbuf0)
    exchange(sent, 1, job_row, job_chan, gated.at[0], gbuf0)
    build(0, gbuf0, 0, False)
    window(wc, cacc, here)
    window(wc, cacc, lower)
    window(wc, cacc, upper)
    shared_window(1, wc, cacc, 0)
    shared_window(1, wc, cacc, 1)
    shared_window(1, wc, cacc, 2)
    kernel_across(1)
    window(wc, cacc, across)
    shared_window(1, wc, cacc, 3)
    finish_cand(0)

    exchange(push, 2, job_row, job_chan, fresh.at[0], sbuf)
    deliver(0, push)
    acc[...] = jnp.zeros_like(acc)
    cacc[...] = jnp.zeros_like(cacc)
    exchanged(2, sbuf)
    exchange(sent, 2, job_row, job_chan, fresh.at[0], sbuf)
    build(1, sbuf, 0, True)

    def all_windows(buf, total):
        def one(t, carry):
            window(buf, total, t)
            return carry

        lax.fori_loop(0, 8, one, 0)

    all_windows(wg, acc)
    finish_gate(1)
    exchange(push, 3, job_row, job_chan, gated.at[1], gbuf1)
    kernel_sent(0)
    kernel_sent(1)
    exchanged(3, gbuf1)
    exchange(sent, 3, job_row, job_chan, gated.at[1], gbuf1)
    build(1, gbuf1, 0, False)
    all_windows(wc, cacc)
    finish_cand(1)
    deliver(1, push)
    for k in range(2):
        arrived(landed.at[k], orecv.at[k])
        out_ref[k] = landed[k]
        deliver(k, sent)


def local(hidden, conditioning, gate_weight, gate_bias, cand_weight, cand_bias):
    state = hidden.reshape(ROWS, OWN, W).transpose(0, 2, 1).reshape(CELLS, OWN)
    cond = conditioning.reshape(2, ROWS, COND, W).transpose(1, 3, 0, 2).reshape(CELLS, 2 * COND)
    act = jnp.concatenate(
        [cond, jnp.zeros((CELLS, 32), BF), state, jnp.zeros((CELLS, 64), BF)], axis=1
    )
    bias = jnp.concatenate([gate_bias, cand_bias[None]], axis=0)
    bias = jnp.pad(bias, ((0, 5), (0, 64)))
    vmem = pl.BlockSpec(memory_space=pltpu.VMEM)
    dma = pltpu.SemaphoreType.DMA
    out = pl.pallas_call(
        kernel,
        out_shape=jax.ShapeDtypeStruct((2, CELLS, OWN), BF),
        in_specs=[vmem] * 4,
        out_specs=vmem,
        scratch_shapes=[
            pltpu.VMEM((8, HALO, 384), BF),
            pltpu.VMEM((8, HALO, OWN), BF),
            pltpu.VMEM((8, HALO, OWN), BF),
            pltpu.VMEM((8, HALO, OWN), BF),
            pltpu.VMEM((8, 9, 4, SLOT, 2 * OWN), BF),
            pltpu.VMEM((8, 9, 4, SLOT, OWN), BF),
            pltpu.VMEM((HALO, 8 * 768), BF),
            pltpu.VMEM((len(PAIRS), OWN, WIN), BF),
            pltpu.VMEM((CELLS, 2 * OWN), F32),
            pltpu.VMEM((CELLS, OWN), F32),
            pltpu.VMEM((CELLS, OWN), F32),
            pltpu.VMEM((CELLS, OWN), F32),
            pltpu.VMEM((2, CELLS, OWN), BF),
            pltpu.VMEM((2, CELLS, OWN), BF),
            pltpu.VMEM((2, CELLS, OWN), BF),
            pltpu.VMEM((8, 256), F32),
            dma((24,)),
            dma((4, 3, 8)),
            dma((2, 32)),
            dma((2, 4)),
            dma((2, 4)),
            dma((2, 4)),
            dma((2, 4)),
            dma((2, 4, 4)),
            dma((2,)),
            dma((2,)),
            dma((2,)),
        ],
        compiler_params=pltpu.CompilerParams(
            collective_id=0, has_side_effects=True, vmem_limit_bytes=63 * 1024 * 1024
        ),
    )(act, gate_taps(gate_weight), cand_taps(cand_weight), bias)
    frames = out.reshape(2, ROWS, W, OWN).transpose(0, 1, 3, 2)
    return frames.reshape(2, ROWS, OWN * W)


def solution(mesh):
    placed = (
        P("space", "chan"),
        P(None, "space", "chan"),
        P("space", "chan"),
        P(None, "chan"),
        P("space", "chan"),
        P("chan"),
    )
    return jax.shard_map(
        local, mesh=mesh, in_specs=placed, out_specs=P(None, "space", "chan"), check_vma=False
    )
```

```python
import functools

import jax
import jax.numpy as jnp
from jax import lax
from jax.experimental import pallas as pl
from jax.experimental.pallas import tpu as pltpu
from jax.sharding import PartitionSpec as P

W = 96
ROWS = 3
CELLS = ROWS * W
HALO = (ROWS + 2) * W
OWN = 192
COND = 48
SHARD = 60
SLOT = 64
WIN = 256
BF = jnp.bfloat16
F32 = jnp.float32
PAIRS = tuple(
    (t, n)
    for t in range(1, 8)
    for n in range(8)
    if max(240 * t, 384 + 192 * n) < min(240 * t + 240, 576 + 192 * n)
)


def gate_taps(raw):
    taps = raw.reshape(SHARD, OWN, 2, 3, 3).transpose(3, 4, 0, 2, 1).reshape(9, SHARD, 2 * OWN)
    return jnp.pad(taps, ((0, 0), (0, SLOT - SHARD), (0, 0)))


def cand_taps(raw):
    taps = raw.reshape(30, OWN, 2, 9).transpose(3, 2, 0, 1)
    taps = jnp.pad(taps, ((0, 0), (0, 0), (0, 2), (0, 0)))
    return taps.reshape(9, SLOT, OWN)


def kernel(
    act_ref, wg_ref, wc_ref, bias_ref, out_ref,
    init, gbuf0, sbuf, gbuf1, wg, wc, xs, emat, acc, cacc, upd, prev,
    fresh, landed, sib_bias,
    xsend, xrecv, wsend, wz, wl, wr, wo, wd, osem, orecv, bsem,
):
    s = lax.axis_index("space")
    ch = lax.axis_index("chan")
    x, z = s // 8, s % 8
    b, y, c = z % 2, ch // 2, ch % 2
    job_row = s - b + c
    job_chan = 2 * y + b
    right = (x + 1) % 4
    left = (x + 3) % 4
    opposite = (x + 2) % 4

    barrier = pltpu.get_barrier_semaphore()

    def greet(space, chan):
        pl.semaphore_signal(
            barrier, inc=1, device_id=(space, chan), device_id_type=pl.DeviceIdType.MESH
        )

    def greet_line(i, carry):
        space, chan = 8 * x + i // 2, 2 * y + i % 2

        @pl.when(jnp.logical_or(space != s, chan != ch))
        def _():
            greet(space, chan)

        return carry

    lax.fori_loop(0, 16, greet_line, 0)
    greet(8 * right + z, ch)
    greet(8 * left + z, ch)
    up = 2 * ((y + 1) % 4) + c
    down = 2 * ((y + 3) % 4) + c
    greet(s, up)
    greet(s, down)
    first = jnp.logical_and(z < 2, c == 0)
    last = jnp.logical_and(z >= 6, c == 1)

    @pl.when(first)
    def _():
        greet(8 * left + 6 + b, 2 * y + 1)

    @pl.when(last)
    def _():
        greet(8 * right + b, 2 * y)

    pl.semaphore_wait(barrier, 19 + jnp.logical_or(first, last).astype(jnp.int32))

    def remote(src, dst, send, recv, space, chan):
        return pltpu.make_async_remote_copy(
            src_ref=src, dst_ref=dst, send_sem=send, recv_sem=recv,
            device_id=(space, chan), device_id_type=pl.DeviceIdType.MESH,
        )

    def push(src, dst, send, recv, space, chan):
        mine = jnp.logical_and(space == s, chan == ch)

        @pl.when(mine)
        def _():
            pltpu.make_async_copy(src, dst, recv).start()

        @pl.when(jnp.logical_not(mine))
        def _():
            remote(src, dst, send, recv, space, chan).start()

    def sent(src, dst, send, recv, space, chan):
        mine = jnp.logical_and(space == s, chan == ch)

        @pl.when(jnp.logical_not(mine))
        def _():
            remote(src, dst, send, recv, space, chan).wait_send()

    def arrived(dst, recv):
        pltpu.make_async_copy(dst, dst, recv).wait()

    mate = s + 1 - 2 * b
    half = HALO // 2
    blocks = [2 * ((y + d) % 4) + b for d in (0, 3, 1, 2)]
    twins = [2 * ((y + d) % 4) + 1 - b for d in (0, 3, 1, 2)]

    def edge(k, buf, down_edge):
        n = job_chan
        to_row = (job_row + (1 if down_edge else 31)) % 32
        src = buf.at[n, pl.ds(3 * W if down_edge else W, W)]
        dst = buf.at[n, pl.ds(0 if down_edge else 4 * W, W)]
        i = 0 if down_edge else 1
        return remote(src, dst, xsend.at[i], xrecv.at[k, 16 + i],
                      to_row - to_row % 2 + b, 2 * y + to_row % 2)

    def part(buf, which, n):
        return buf.at[n, pl.ds(which * half, half)]

    def move(k, buf, which, n, i, space, chan):
        ref = part(buf, which, n)
        return remote(ref, ref, xsend.at[i], xrecv.at[k, 8 * which + n], space, chan)

    def moves(k, buf):
        own_a = [move(k, buf, 0, blocks[0], 2, s, up), move(k, buf, 0, blocks[0], 3, s, down)]
        own_b = [move(k, buf, 1, blocks[0], 4, mate, ch),
                 move(k, buf, 1, blocks[0], 5, s, up), move(k, buf, 1, blocks[0], 6, s, down)]
        on_a = [move(k, buf, 0, blocks[d], 7 + d, mate, ch) for d in range(4)]
        pass_a = move(k, buf, 0, blocks[1], 11, s, up)
        mate_b = [move(k, buf, 1, twins[0], 12, s, up), move(k, buf, 1, twins[0], 13, s, down)]
        pass_b = [move(k, buf, 1, blocks[2], 14, s, down), move(k, buf, 1, twins[2], 15, s, down)]
        return own_a, own_b, on_a, pass_a, mate_b, pass_b

    def got(k, buf, which, n):
        arrived(part(buf, which, n), xrecv.at[k, 8 * which + n])

    def edges_out(k, buf):
        edge(k, buf, True).start()
        edge(k, buf, False).start()

    def exchange(k, buf):
        own_a, own_b, on_a, pass_a, mate_b, pass_b = moves(k, buf)
        arrived(buf.at[job_chan, pl.ds(0, W)], xrecv.at[k, 16])
        for m in own_a:
            m.start()
        on_a[0].start()
        arrived(buf.at[job_chan, pl.ds(4 * W, W)], xrecv.at[k, 17])
        for m in own_b:
            m.start()
        got(k, buf, 0, blocks[1])
        pass_a.start()
        on_a[1].start()
        got(k, buf, 0, blocks[2])
        on_a[2].start()
        got(k, buf, 1, twins[0])
        for m in mate_b:
            m.start()
        got(k, buf, 1, blocks[2])
        pass_b[0].start()
        got(k, buf, 1, twins[2])
        pass_b[1].start()
        got(k, buf, 0, blocks[3])
        on_a[3].start()

    def exchanged(k, buf):
        for d in range(4):
            got(k, buf, 0, twins[d])
        for d in (1, 3):
            got(k, buf, 1, blocks[d])
            got(k, buf, 1, twins[d])

    def exchange_sent(k, buf):
        own_a, own_b, on_a, pass_a, mate_b, pass_b = moves(k, buf)
        edge(k, buf, True).wait_send()
        edge(k, buf, False).wait_send()
        for m in own_a + own_b + on_a + [pass_a] + mate_b + pass_b:
            m.wait_send()

    def own_rows(buf):
        return buf.at[job_chan, pl.ds(W, CELLS)]

    group = z // 4
    spot = z % 4
    mine = ((wg_ref, wg), (wc_ref, wc))

    def kernel_z(kind, act):
        src, buf = mine[kind]

        def one(i, carry):
            to = (z // 2 + jnp.where(c == 0, i, 4 - i)) % 4
            act(src, buf.at[2 * x + group, :, spot], wsend.at[kind, i], wz.at[kind, spot],
                8 * x + 2 * to + c, 2 * y + group)
            return carry

        lax.fori_loop(0, 4, one, 0)

    lag = (z // 2 + 8 - 2 * c) % 4
    head = jnp.where(b == 0, jnp.where(lag == 0, 0, 2), jnp.where(lag == 1, 2, 0))
    turn = [(i + head) % 4 for i in range(4)]

    here, lower, upper, across = 2 * x + c, 2 * left + c, 2 * right + c, 2 * opposite + c

    def hop(kind, t, i, send, recv, space, chan):
        buf = mine[kind][1]
        return remote(buf.at[t, :, i], buf.at[t, :, i], wsend.at[kind, send], recv, space, chan)

    def go_right(kind, i):
        return hop(kind, here, i, 4 + i, wl.at[kind, i], 8 * right + z, ch)

    def go_left(kind, i):
        return hop(kind, here, i, 8 + i, wr.at[kind, i], 8 * left + z, ch)

    def pass_right(kind, i):
        return hop(kind, lower, i, 12 + i, wo.at[kind, i], 8 * right + z, ch)

    def pass_left(kind, i):
        return hop(kind, upper, i, 12 + i, wo.at[kind, i], 8 * left + z, ch)

    def share(kind, j, i):
        t = (here, lower, upper, across)[j]
        return hop(kind, t, i, 16 + 4 * j + i, wd.at[kind, j, i], s, 2 * y + 1 - c)

    def piece(kind, t, i):
        return mine[kind][1].at[t, :, i]

    def kernel_own(kind):
        for parity, i in zip((0, 1, 0, 1), turn):
            arrived(piece(kind, here, i), wz.at[kind, i])
            go_right(kind, i).start()
            go_left(kind, i).start()
            share(kind, 0, i).start()

    def kernel_sides(kind):
        for parity, i in zip((0, 1, 0, 1), turn):
            arrived(piece(kind, lower, i), wl.at[kind, i])
            if parity == 0:
                pass_right(kind, i).start()
            share(kind, 1, i).start()
            arrived(piece(kind, upper, i), wr.at[kind, i])
            if parity == 1:
                pass_left(kind, i).start()
            share(kind, 2, i).start()

    def kernel_across(kind):
        for parity, i in zip((0, 1, 0, 1), turn):
            arrived(piece(kind, across, i), wo.at[kind, i])
            share(kind, 3, i).start()

    def kernel_shared(kind, j):
        t = 2 * ((here, lower, upper, across)[j] // 2) + 1 - c
        for i in range(4):
            arrived(piece(kind, t, i), wd.at[kind, j, i])
        return t

    def kernel_sent(kind):
        kernel_z(kind, sent)
        for i in range(4):
            go_right(kind, i).wait_send()
            go_left(kind, i).wait_send()
            if i % 2 == 0:
                pass_right(kind, i).wait_send()
            else:
                pass_left(kind, i).wait_send()
            for j in range(4):
                share(kind, j, i).wait_send()

    def slot_channel(order, t, rows):
        j = lax.broadcasted_iota(jnp.int32, (rows, WIN), 1)
        r = j % SLOT
        base = SHARD * (4 * t + j // SLOT)
        if order == 0:
            return jnp.where(r < SHARD, base + r, -1)
        m = r % 32
        return jnp.where(m < 30, base + 2 * m + r // 32, -1)

    def spread(t, v):
        cell = lax.broadcasted_iota(jnp.int32, (HALO, WIN), 0)
        col = cell % W
        inside = jnp.logical_and(
            jnp.logical_or(cell >= W, job_row > 0),
            jnp.logical_or(cell < 4 * W, job_row < 31),
        )
        v = jnp.where(inside, v, 0.0)
        low = jnp.where(col == 0, 0.0, pltpu.roll(v, 1, 0))
        high = jnp.where(col == W - 1, 0.0, pltpu.roll(v, HALO - 1, 0))
        xs[:, 768 * t:768 * t + 256] = low.astype(BF)
        xs[:, 768 * t + 256:768 * t + 512] = v.astype(BF)
        xs[:, 768 * t + 512:768 * t + 768] = high.astype(BF)

    def cond_slots(step, order, t):
        v = jnp.zeros((HALO, WIN), F32)
        lane = lax.broadcasted_iota(jnp.int32, (128, WIN), 0)
        want = slot_channel(order, t, 128)
        for n in range(5 * t, min(8, 5 * t + 5)):
            here_n = jnp.logical_and(lane >= COND * step, lane < COND * step + COND)
            hit = jnp.logical_and(here_n, want == COND * n + lane - COND * step)
            e = hit.astype(F32).astype(BF)
            v = v + jnp.dot(init[n, :, 0:128], e, preferred_element_type=F32)
        return v

    def build(step, order, buf, base):
        spread(0, cond_slots(step, order, 0))
        for t in range(1, 8):
            v = cond_slots(step, order, 1) if t == 1 else jnp.zeros((HALO, WIN), F32)
            for q, (pt, n) in enumerate(PAIRS):
                if pt == t:
                    v = v + jnp.dot(buf[n, :, base:base + OWN], emat[order, q], preferred_element_type=F32)
            spread(t, v)

    def window(buf, total, t):
        lane = pl.multiple_of(768 * t, 768)
        out = total.shape[1]
        for a in range(3):
            total[...] += jnp.dot(
                xs[pl.ds(a * W, CELLS), pl.ds(lane, 768)],
                buf[t, 3 * a:3 * a + 3].reshape(768, out),
                preferred_element_type=F32,
            )

    def bias(row):
        return jnp.where(b == c, bias_ref[row:row + 1, 0:OWN], sib_bias[row:row + 1, 0:OWN])

    def finish_gate(buf):
        pre = acc[...]
        upd[...] = jax.nn.sigmoid(pre[:, :OWN] + bias(0))
        reset = jax.nn.sigmoid(pltpu.roll(pre, OWN, 1)[:, :OWN] + bias(1))
        buf[job_chan, pl.ds(W, CELLS), :] = (reset * prev[...]).astype(BF)

    def finish_cand(k):
        candidate = jnp.tanh(cacc[...] + bias(2))
        u = upd[...]
        new = ((1.0 - u) * prev[...] + u * candidate).astype(BF)
        fresh[k] = new
        prev[...] = new.astype(F32)

    def deliver(k, act):
        act(fresh.at[k], landed.at[k], osem.at[k], orecv.at[k], job_row, job_chan)

    kernel_z(0, push)
    first_copy = (act_ref, init.at[ch, pl.ds(W, CELLS)], bsem.at[2], bsem.at[3], job_row, job_chan)
    push(*first_copy)
    bias_copy = remote(bias_ref, sib_bias, bsem.at[0], bsem.at[1], s, 2 * y + 1 - c)
    bias_copy.start()
    arrived(own_rows(init), bsem.at[3])
    edges_out(0, init)
    kernel_z(1, push)
    for order in range(2):
        for q, (t, n) in enumerate(PAIRS):
            lane = lax.broadcasted_iota(jnp.int32, (OWN, WIN), 0)
            hit = slot_channel(order, t, OWN) == 384 + 192 * n + lane
            emat[order, q] = hit.astype(F32).astype(BF)
    acc[...] = jnp.zeros_like(acc)
    cacc[...] = jnp.zeros_like(cacc)
    kernel_own(0)
    exchange(0, init)
    kernel_sides(0)
    kernel_own(1)
    sent(*first_copy)
    bias_copy.wait()
    exchanged(0, init)
    prev[...] = init[job_chan, pl.ds(W, CELLS), 128:128 + OWN].astype(F32)
    build(0, 0, init, 128)

    def shared_window(kind, buf, total, j):
        window(buf, total, kernel_shared(kind, j))

    window(wg, acc, here)
    window(wg, acc, lower)
    window(wg, acc, upper)
    shared_window(0, wg, acc, 0)
    shared_window(0, wg, acc, 1)
    shared_window(0, wg, acc, 2)
    kernel_across(0)
    window(wg, acc, across)
    shared_window(0, wg, acc, 3)
    exchange_sent(0, init)
    finish_gate(gbuf0)
    edges_out(1, gbuf0)
    exchange(1, gbuf0)
    kernel_sides(1)
    exchanged(1, gbuf0)
    build(0, 1, gbuf0, 0)
    window(wc, cacc, here)
    window(wc, cacc, lower)
    window(wc, cacc, upper)
    shared_window(1, wc, cacc, 0)
    shared_window(1, wc, cacc, 1)
    shared_window(1, wc, cacc, 2)
    kernel_across(1)
    window(wc, cacc, across)
    shared_window(1, wc, cacc, 3)
    exchange_sent(1, gbuf0)
    finish_cand(0)

    sbuf[job_chan, pl.ds(W, CELLS), :] = fresh[0]
    edges_out(2, sbuf)
    deliver(0, push)
    acc[...] = jnp.zeros_like(acc)
    cacc[...] = jnp.zeros_like(cacc)
    exchange(2, sbuf)
    exchanged(2, sbuf)
    build(1, 0, sbuf, 0)

    def all_windows(buf, total):
        def one(t, carry):
            window(buf, total, t)
            return carry

        lax.fori_loop(0, 8, one, 0)

    all_windows(wg, acc)
    exchange_sent(2, sbuf)
    finish_gate(gbuf1)
    edges_out(3, gbuf1)
    exchange(3, gbuf1)
    kernel_sent(0)
    kernel_sent(1)
    exchanged(3, gbuf1)
    build(1, 1, gbuf1, 0)
    all_windows(wc, cacc)
    exchange_sent(3, gbuf1)
    finish_cand(1)
    deliver(1, push)
    for k in range(2):
        arrived(landed.at[k], orecv.at[k])
        out_ref[k] = landed[k]
        deliver(k, sent)


def local(hidden, conditioning, gate_weight, gate_bias, cand_weight, cand_bias):
    state = hidden.reshape(ROWS, OWN, W).transpose(0, 2, 1).reshape(CELLS, OWN)
    cond = conditioning.reshape(2, ROWS, COND, W).transpose(1, 3, 0, 2).reshape(CELLS, 2 * COND)
    act = jnp.concatenate(
        [cond, jnp.zeros((CELLS, 32), BF), state, jnp.zeros((CELLS, 64), BF)], axis=1
    )
    bias = jnp.concatenate([gate_bias, cand_bias[None]], axis=0)
    bias = jnp.pad(bias, ((0, 5), (0, 64)))
    vmem = pl.BlockSpec(memory_space=pltpu.VMEM)
    dma = pltpu.SemaphoreType.DMA
    out = pl.pallas_call(
        kernel,
        out_shape=jax.ShapeDtypeStruct((2, CELLS, OWN), BF),
        in_specs=[vmem] * 4,
        out_specs=vmem,
        scratch_shapes=[
            pltpu.VMEM((8, HALO, 384), BF),
            pltpu.VMEM((8, HALO, OWN), BF),
            pltpu.VMEM((8, HALO, OWN), BF),
            pltpu.VMEM((8, HALO, OWN), BF),
            pltpu.VMEM((8, 9, 4, SLOT, 2 * OWN), BF),
            pltpu.VMEM((8, 9, 4, SLOT, OWN), BF),
            pltpu.VMEM((HALO, 8 * 768), BF),
            pltpu.VMEM((2, len(PAIRS), OWN, WIN), BF),
            pltpu.VMEM((CELLS, 2 * OWN), F32),
            pltpu.VMEM((CELLS, OWN), F32),
            pltpu.VMEM((CELLS, OWN), F32),
            pltpu.VMEM((CELLS, OWN), F32),
            pltpu.VMEM((2, CELLS, OWN), BF),
            pltpu.VMEM((2, CELLS, OWN), BF),
            pltpu.VMEM((8, 256), F32),
            dma((16,)),
            dma((4, 18)),
            dma((2, 32)),
            dma((2, 4)),
            dma((2, 4)),
            dma((2, 4)),
            dma((2, 4)),
            dma((2, 4, 4)),
            dma((2,)),
            dma((2,)),
            dma((4,)),
        ],
        compiler_params=pltpu.CompilerParams(
            collective_id=0, has_side_effects=True, vmem_limit_bytes=63 * 1024 * 1024
        ),
    )(act, gate_taps(gate_weight), cand_taps(cand_weight), bias)
    frames = out.reshape(2, ROWS, W, OWN).transpose(0, 1, 3, 2)
    return frames.reshape(2, ROWS, OWN * W)


def solution(mesh):
    placed = (
        P("space", "chan"),
        P(None, "space", "chan"),
        P("space", "chan"),
        P(None, "chan"),
        P("space", "chan"),
        P("chan"),
    )
    return jax.shard_map(
        local, mesh=mesh, in_specs=placed, out_specs=P(None, "space", "chan"), check_vma=False
    )
```

```python
import functools

import jax
import jax.numpy as jnp
from jax import lax
from jax.experimental import pallas as pl
from jax.experimental.pallas import tpu as pltpu
from jax.sharding import PartitionSpec as P

W = 96
ROWS = 3
CELLS = ROWS * W
HALO = (ROWS + 2) * W
OWN = 192
COND = 48
SHARD = 60
SLOT = 64
WIN = 256
BF = jnp.bfloat16
F32 = jnp.float32
PAIRS = tuple(
    (t, n)
    for t in range(1, 8)
    for n in range(8)
    if max(240 * t, 384 + 192 * n) < min(240 * t + 240, 576 + 192 * n)
)


def gate_taps(raw):
    taps = raw.reshape(SHARD, OWN, 2, 3, 3).transpose(3, 4, 0, 2, 1).reshape(9, SHARD, 2 * OWN)
    return jnp.pad(taps, ((0, 0), (0, SLOT - SHARD), (0, 0)))


def cand_taps(raw):
    taps = raw.reshape(30, OWN, 2, 9).transpose(3, 2, 0, 1)
    taps = jnp.pad(taps, ((0, 0), (0, 0), (0, 2), (0, 0)))
    return jnp.concatenate([taps[:, 0], taps[:, 1]], axis=2)


def kernel(
    act_ref, wg_ref, wc_ref, bias_ref, out_ref,
    init, gbuf0, sbuf, gbuf1, wg, wc, xs, emat, acc, cacc, upd, prev,
    fresh, landed, sib_bias,
    xsend, xrecv, wsend, wz, wl, wr, wo, wd, osem, orecv, bsem,
):
    s = lax.axis_index("space")
    ch = lax.axis_index("chan")
    x, z = s // 8, s % 8
    b, y, c = z % 2, ch // 2, ch % 2
    job_row = s - b + c
    job_chan = 2 * y + b
    right = (x + 1) % 4
    left = (x + 3) % 4
    opposite = (x + 2) % 4

    barrier = pltpu.get_barrier_semaphore()

    def greet(space, chan):
        pl.semaphore_signal(
            barrier, inc=1, device_id=(space, chan), device_id_type=pl.DeviceIdType.MESH
        )

    def greet_line(i, carry):
        space, chan = 8 * x + i // 2, 2 * y + i % 2

        @pl.when(jnp.logical_or(space != s, chan != ch))
        def _():
            greet(space, chan)

        return carry

    lax.fori_loop(0, 16, greet_line, 0)
    greet(8 * right + z, ch)
    greet(8 * left + z, ch)
    up = 2 * ((y + 1) % 4) + c
    down = 2 * ((y + 3) % 4) + c
    greet(s, up)
    greet(s, down)
    first = jnp.logical_and(z < 2, c == 0)
    last = jnp.logical_and(z >= 6, c == 1)

    @pl.when(first)
    def _():
        greet(8 * left + 6 + b, 2 * y + 1)

    @pl.when(last)
    def _():
        greet(8 * right + b, 2 * y)

    pl.semaphore_wait(barrier, 19 + jnp.logical_or(first, last).astype(jnp.int32))

    def remote(src, dst, send, recv, space, chan):
        return pltpu.make_async_remote_copy(
            src_ref=src, dst_ref=dst, send_sem=send, recv_sem=recv,
            device_id=(space, chan), device_id_type=pl.DeviceIdType.MESH,
        )

    def push(src, dst, send, recv, space, chan):
        mine = jnp.logical_and(space == s, chan == ch)

        @pl.when(mine)
        def _():
            pltpu.make_async_copy(src, dst, recv).start()

        @pl.when(jnp.logical_not(mine))
        def _():
            remote(src, dst, send, recv, space, chan).start()

    def sent(src, dst, send, recv, space, chan):
        mine = jnp.logical_and(space == s, chan == ch)

        @pl.when(jnp.logical_not(mine))
        def _():
            remote(src, dst, send, recv, space, chan).wait_send()

    def arrived(dst, recv):
        pltpu.make_async_copy(dst, dst, recv).wait()

    mate = s + 1 - 2 * b
    spans = ((W, CELLS // 2), (W + CELLS // 2, CELLS // 2), (0, W), (4 * W, W))
    blocks = [2 * ((y + d) % 4) + b for d in (0, 3, 1, 2)]
    twins = [2 * ((y + d) % 4) + 1 - b for d in (0, 3, 1, 2)]

    def edge(k, buf, down_edge):
        n = job_chan
        to_row = (job_row + (1 if down_edge else 31)) % 32
        src = buf.at[n, pl.ds(3 * W if down_edge else W, W)]
        dst = buf.at[n, pl.ds(0 if down_edge else 4 * W, W)]
        i = 0 if down_edge else 1
        return remote(src, dst, xsend.at[i], xrecv.at[k, 32 + i],
                      to_row - to_row % 2 + b, 2 * y + to_row % 2)

    def part(buf, which, n):
        return buf.at[n, pl.ds(*spans[which])]

    def move(k, buf, which, n, i, space, chan):
        ref = part(buf, which, n)
        send = xsend.at[2 + 14 * (which // 2) + i]
        return remote(ref, ref, send, xrecv.at[k, 8 * which + n], space, chan)

    def moves(k, buf, g):
        p, q = 2 * g, 2 * g + 1
        own_a = [move(k, buf, p, blocks[0], 0, s, up), move(k, buf, p, blocks[0], 1, s, down)]
        own_b = [move(k, buf, q, blocks[0], 2, mate, ch),
                 move(k, buf, q, blocks[0], 3, s, up), move(k, buf, q, blocks[0], 4, s, down)]
        on_a = [move(k, buf, p, blocks[d], 5 + d, mate, ch) for d in range(4)]
        pass_a = move(k, buf, p, blocks[1], 9, s, up)
        mate_b = [move(k, buf, q, twins[0], 10, s, up), move(k, buf, q, twins[0], 11, s, down)]
        pass_b = [move(k, buf, q, blocks[2], 12, s, down), move(k, buf, q, twins[2], 13, s, down)]
        return own_a, own_b, on_a, pass_a, mate_b, pass_b

    def got(k, buf, which, n):
        arrived(part(buf, which, n), xrecv.at[k, 8 * which + n])

    def edges_out(k, buf):
        edge(k, buf, True).start()
        edge(k, buf, False).start()

    def exchange_own(k, buf, g):
        own_a, own_b, on_a, _, _, _ = moves(k, buf, g)
        if g == 1:
            arrived(part(buf, 2, job_chan), xrecv.at[k, 32])
            arrived(part(buf, 3, job_chan), xrecv.at[k, 33])
        for m in [own_b[0]] + own_a + [on_a[0]] + own_b[1:]:
            m.start()

    def exchange_on(k, buf, g):
        _, _, on_a, pass_a, mate_b, pass_b = moves(k, buf, g)
        p, q = 2 * g, 2 * g + 1
        got(k, buf, q, twins[0])
        for m in mate_b:
            m.start()
        got(k, buf, p, blocks[1])
        pass_a.start()
        on_a[1].start()
        got(k, buf, p, blocks[2])
        on_a[2].start()
        got(k, buf, q, blocks[2])
        pass_b[0].start()
        got(k, buf, q, twins[2])
        pass_b[1].start()

    def exchange(k, buf):
        exchange_own(k, buf, 0)
        exchange_own(k, buf, 1)
        exchange_rest(k, buf)

    def exchange_rest(k, buf):
        exchange_on(k, buf, 0)
        exchange_on(k, buf, 1)
        for g in range(2):
            got(k, buf, 2 * g, blocks[3])
            moves(k, buf, g)[2][3].start()

    def exchanged(k, buf):
        for g in range(2):
            for d in range(4):
                got(k, buf, 2 * g, twins[d])
            for d in (1, 3):
                got(k, buf, 2 * g + 1, blocks[d])
                got(k, buf, 2 * g + 1, twins[d])

    def exchange_sent(k, buf):
        edge(k, buf, True).wait_send()
        edge(k, buf, False).wait_send()
        for g in range(2):
            own_a, own_b, on_a, pass_a, mate_b, pass_b = moves(k, buf, g)
            for m in own_a + own_b + on_a + [pass_a] + mate_b + pass_b:
                m.wait_send()

    def own_rows(buf):
        return buf.at[job_chan, pl.ds(W, CELLS)]

    group = z // 4
    spot = z % 4
    mine = ((wg_ref, wg), (wc_ref, wc))

    def kernel_z(kind, act, i):
        src, buf = mine[kind]
        to = (z // 2 + (0 if i == 0 else jnp.where(c == 0, i, 4 - i))) % 4
        act(src, buf.at[2 * x + group, :, spot], wsend.at[kind, i], wz.at[kind, spot],
            8 * x + 2 * to + c, 2 * y + group)

    lag = (z // 2 + 8 - 2 * c) % 4
    head = jnp.where(b == 0, jnp.where(lag == 0, 0, 2), jnp.where(lag == 1, 2, 0))
    turn = [(i + head) % 4 for i in range(4)]

    here, lower, upper, across = 2 * x + c, 2 * left + c, 2 * right + c, 2 * opposite + c

    def hop(kind, t, i, send, recv, space, chan):
        buf = mine[kind][1]
        return remote(buf.at[t, :, i], buf.at[t, :, i], wsend.at[kind, send], recv, space, chan)

    def go_right(kind, i):
        return hop(kind, here, i, 4 + i, wl.at[kind, i], 8 * right + z, ch)

    def go_left(kind, i):
        return hop(kind, here, i, 8 + i, wr.at[kind, i], 8 * left + z, ch)

    def pass_right(kind, i):
        return hop(kind, lower, i, 12 + i, wo.at[kind, i], 8 * right + z, ch)

    def pass_left(kind, i):
        return hop(kind, upper, i, 12 + i, wo.at[kind, i], 8 * left + z, ch)

    def share(kind, j, i):
        t = (here, lower, upper, across)[j]
        return hop(kind, t, i, 16 + 4 * j + i, wd.at[kind, j, i], s, 2 * y + 1 - c)

    def piece(kind, t, i):
        return mine[kind][1].at[t, :, i]

    def onward(kind, parity, i):
        return hop(kind, here, i, 2 if parity == 0 else 32, wz.at[kind, i],
                   8 * x + (z + jnp.where(b == 0, 2, 6)) % 8, ch)

    def passes_on(i):
        source = 2 * c + i // 2
        steps = jnp.where(b == 0, z // 2 - source + 4, source - z // 2 + 4) % 4
        return steps == 1

    def kernel_relay(kind):
        for parity, i in zip((0, 1, 0, 1), turn):
            @pl.when(passes_on(i))
            def _():
                arrived(piece(kind, here, i), wz.at[kind, i])
                onward(kind, parity, i).start()

    def kernel_own(kind, relayed, pair):
        for parity, i in zip((0, 1), turn[2 * pair:2 * pair + 2]):
            if relayed:
                @pl.when(jnp.logical_not(passes_on(i)))
                def _():
                    arrived(piece(kind, here, i), wz.at[kind, i])
            else:
                arrived(piece(kind, here, i), wz.at[kind, i])

                @pl.when(passes_on(i))
                def _():
                    onward(kind, parity, i).start()
            go_right(kind, i).start()
            go_left(kind, i).start()
            share(kind, 0, i).start()

    def kernel_sides(kind, pair):
        for parity, i in zip((0, 1), turn[2 * pair:2 * pair + 2]):
            arrived(piece(kind, lower, i), wl.at[kind, i])
            if parity == 0:
                pass_right(kind, i).start()
            share(kind, 1, i).start()
            arrived(piece(kind, upper, i), wr.at[kind, i])
            if parity == 1:
                pass_left(kind, i).start()
            share(kind, 2, i).start()

    def kernel_across(kind):
        for parity, i in zip((0, 1, 0, 1), turn):
            arrived(piece(kind, across, i), wo.at[kind, i])
            share(kind, 3, i).start()

    def kernel_shared(kind, j):
        t = 2 * ((here, lower, upper, across)[j] // 2) + 1 - c
        for i in range(4):
            arrived(piece(kind, t, i), wd.at[kind, j, i])
        return t

    def kernel_sent(kind):
        for i in (0, 3) if kind == 0 else (0, 1, 3):
            kernel_z(kind, sent, i)
        for parity, i in zip((0, 1, 0, 1), turn):
            @pl.when(passes_on(i))
            def _():
                onward(kind, parity, i).wait_send()
        for i in range(4):
            go_right(kind, i).wait_send()
            go_left(kind, i).wait_send()
            if i % 2 == 0:
                pass_right(kind, i).wait_send()
            else:
                pass_left(kind, i).wait_send()
            for j in range(4):
                share(kind, j, i).wait_send()

    def slot_channel(order, t, rows):
        j = lax.broadcasted_iota(jnp.int32, (rows, WIN), 1)
        if order == 0:
            r = j % SLOT
            return jnp.where(r < SHARD, SHARD * (4 * t + j // SLOT) + r, -1)
        m = j % 32
        return jnp.where(m < 30, SHARD * (4 * t + j % 128 // 32) + 2 * m + j // 128, -1)

    def spread(order, t, v):
        cell = lax.broadcasted_iota(jnp.int32, (HALO, WIN), 0)
        col = cell % W
        inside = jnp.logical_and(
            jnp.logical_or(cell >= W, job_row > 0),
            jnp.logical_or(cell < 4 * W, job_row < 31),
        )
        v = jnp.where(inside, v, 0.0)
        low = jnp.where(col == 0, 0.0, pltpu.roll(v, 1, 0))
        high = jnp.where(col == W - 1, 0.0, pltpu.roll(v, HALO - 1, 0))
        for d, shifted in enumerate((low, v, high)):
            shifted = shifted.astype(BF)
            if order == 0:
                xs[:, 768 * t + 256 * d:768 * t + 256 * d + 256] = shifted
            else:
                for p in range(2):
                    at = 768 * t + 384 * p + 128 * d
                    xs[:, at:at + 128] = shifted[:, 128 * p:128 * p + 128]

    def cond_slots(step, order, t):
        v = jnp.zeros((HALO, WIN), F32)
        lane = lax.broadcasted_iota(jnp.int32, (128, WIN), 0)
        want = slot_channel(order, t, 128)
        for n in range(5 * t, min(8, 5 * t + 5)):
            here_n = jnp.logical_and(lane >= COND * step, lane < COND * step + COND)
            hit = jnp.logical_and(here_n, want == COND * n + lane - COND * step)
            e = hit.astype(F32).astype(BF)
            v = v + jnp.dot(init[n, :, 0:128], e, preferred_element_type=F32)
        return v

    def build(step, order, buf, base):
        spread(order, 0, cond_slots(step, order, 0))
        for t in range(1, 8):
            v = cond_slots(step, order, 1) if t == 1 else jnp.zeros((HALO, WIN), F32)
            for q, (pt, n) in enumerate(PAIRS):
                if pt == t:
                    v = v + jnp.dot(buf[n, :, base:base + OWN], emat[order, q], preferred_element_type=F32)
            spread(order, t, v)

    def window(buf, total, t):
        depth = 2 * OWN if total is cacc else 768
        for p in range(768 // depth):
            lane = pl.multiple_of(768 * t + depth * p, depth)
            sums = total.at[p] if total is cacc else total
            for a in range(3):
                sums[...] += jnp.dot(
                    xs[pl.ds(a * W, CELLS), pl.ds(lane, depth)],
                    buf[t, 3 * a:3 * a + 3].reshape(depth, 2 * OWN),
                    preferred_element_type=F32,
                )

    def bias(row):
        return jnp.where(b == c, bias_ref[row:row + 1, 0:OWN], sib_bias[row:row + 1, 0:OWN])

    def finish_gate(buf):
        pre = acc[...]
        upd[...] = jax.nn.sigmoid(pre[:, :OWN] + bias(0))
        reset = jax.nn.sigmoid(pltpu.roll(pre, OWN, 1)[:, :OWN] + bias(1))
        buf[job_chan, pl.ds(W, CELLS), :] = (reset * prev[...]).astype(BF)

    def finish_cand(k):
        candidate = jnp.tanh(cacc[0][:, :OWN] + pltpu.roll(cacc[1], OWN, 1)[:, :OWN] + bias(2))
        u = upd[...]
        new = ((1.0 - u) * prev[...] + u * candidate).astype(BF)
        fresh[k] = new
        prev[...] = new.astype(F32)

    def deliver(k, act):
        act(fresh.at[k], landed.at[k], osem.at[k], orecv.at[k], job_row, job_chan)

    def kernel_z_rest():
        kernel_z(0, sent, 1)
        kernel_z(0, push, 3)

    kernel_z(0, push, 0)
    kernel_z(0, push, 1)
    first_copy = (act_ref, init.at[ch, pl.ds(W, CELLS)], bsem.at[2], bsem.at[3], job_row, job_chan)
    push(*first_copy)
    bias_copy = remote(bias_ref, sib_bias, bsem.at[0], bsem.at[1], s, 2 * y + 1 - c)
    bias_copy.start()
    late = jnp.where(b == 0, lag, (4 - lag) % 4) == jnp.where(b == 0, 3, 2)
    pl.when(late)(kernel_z_rest)
    kernel_own(0, False, 0)
    pl.when(jnp.logical_not(late))(kernel_z_rest)
    arrived(own_rows(init), bsem.at[3])
    edges_out(0, init)
    kernel_own(0, False, 1)
    for i in (0, 1, 3):
        kernel_z(1, push, i)
    exchange_own(0, init, 0)
    exchange_own(0, init, 1)
    kernel_sides(0, 0)
    for order in range(2):
        for q, (t, n) in enumerate(PAIRS):
            lane = lax.broadcasted_iota(jnp.int32, (OWN, WIN), 0)
            hit = slot_channel(order, t, OWN) == 384 + 192 * n + lane
            emat[order, q] = hit.astype(F32).astype(BF)
    acc[...] = jnp.zeros_like(acc)
    cacc[...] = jnp.zeros_like(cacc)
    exchange_rest(0, init)
    kernel_relay(1)
    kernel_sides(0, 1)
    kernel_own(1, True, 0)
    kernel_own(1, True, 1)
    sent(*first_copy)
    bias_copy.wait()
    exchanged(0, init)
    prev[...] = init[job_chan, pl.ds(W, CELLS), 128:128 + OWN].astype(F32)
    build(0, 0, init, 128)

    def shared_window(kind, buf, total, j):
        window(buf, total, kernel_shared(kind, j))

    window(wg, acc, here)
    window(wg, acc, lower)
    window(wg, acc, upper)
    shared_window(0, wg, acc, 0)
    shared_window(0, wg, acc, 1)
    shared_window(0, wg, acc, 2)
    kernel_across(0)
    window(wg, acc, across)
    shared_window(0, wg, acc, 3)
    exchange_sent(0, init)
    finish_gate(gbuf0)
    edges_out(1, gbuf0)
    exchange(1, gbuf0)
    kernel_sides(1, 0)
    kernel_sides(1, 1)
    exchanged(1, gbuf0)
    build(0, 1, gbuf0, 0)
    window(wc, cacc, here)
    window(wc, cacc, lower)
    window(wc, cacc, upper)
    shared_window(1, wc, cacc, 0)
    shared_window(1, wc, cacc, 1)
    shared_window(1, wc, cacc, 2)
    kernel_across(1)
    window(wc, cacc, across)
    shared_window(1, wc, cacc, 3)
    exchange_sent(1, gbuf0)
    finish_cand(0)

    sbuf[job_chan, pl.ds(W, CELLS), :] = fresh[0]
    edges_out(2, sbuf)
    deliver(0, push)
    acc[...] = jnp.zeros_like(acc)
    cacc[...] = jnp.zeros_like(cacc)
    exchange(2, sbuf)
    exchanged(2, sbuf)
    build(1, 0, sbuf, 0)

    def all_windows(buf, total):
        def one(t, carry):
            window(buf, total, t)
            return carry

        lax.fori_loop(0, 8, one, 0)

    all_windows(wg, acc)
    exchange_sent(2, sbuf)
    finish_gate(gbuf1)
    edges_out(3, gbuf1)
    exchange(3, gbuf1)
    kernel_sent(0)
    kernel_sent(1)
    exchanged(3, gbuf1)
    build(1, 1, gbuf1, 0)
    all_windows(wc, cacc)
    exchange_sent(3, gbuf1)
    finish_cand(1)
    deliver(1, push)
    for k in range(2):
        arrived(landed.at[k], orecv.at[k])
        out_ref[k] = landed[k]
        deliver(k, sent)


def local(hidden, conditioning, gate_weight, gate_bias, cand_weight, cand_bias):
    state = hidden.reshape(ROWS, OWN, W).transpose(0, 2, 1).reshape(CELLS, OWN)
    cond = conditioning.reshape(2, ROWS, COND, W).transpose(1, 3, 0, 2).reshape(CELLS, 2 * COND)
    act = jnp.concatenate(
        [cond, jnp.zeros((CELLS, 32), BF), state, jnp.zeros((CELLS, 64), BF)], axis=1
    )
    bias = jnp.concatenate([gate_bias, cand_bias[None]], axis=0)
    bias = jnp.pad(bias, ((0, 5), (0, 64)))
    vmem = pl.BlockSpec(memory_space=pltpu.VMEM)
    dma = pltpu.SemaphoreType.DMA
    out = pl.pallas_call(
        kernel,
        out_shape=jax.ShapeDtypeStruct((2, CELLS, OWN), BF),
        in_specs=[vmem] * 4,
        out_specs=vmem,
        scratch_shapes=[
            pltpu.VMEM((8, HALO, 384), BF),
            pltpu.VMEM((8, HALO, OWN), BF),
            pltpu.VMEM((8, HALO, OWN), BF),
            pltpu.VMEM((8, HALO, OWN), BF),
            pltpu.VMEM((8, 9, 4, SLOT, 2 * OWN), BF),
            pltpu.VMEM((8, 9, 4, SLOT // 2, 2 * OWN), BF),
            pltpu.VMEM((HALO, 8 * 768), BF),
            pltpu.VMEM((2, len(PAIRS), OWN, WIN), BF),
            pltpu.VMEM((CELLS, 2 * OWN), F32),
            pltpu.VMEM((2, CELLS, 2 * OWN), F32),
            pltpu.VMEM((CELLS, OWN), F32),
            pltpu.VMEM((CELLS, OWN), F32),
            pltpu.VMEM((2, CELLS, OWN), BF),
            pltpu.VMEM((2, CELLS, OWN), BF),
            pltpu.VMEM((8, 256), F32),
            dma((30,)),
            dma((4, 34)),
            dma((2, 33)),
            dma((2, 4)),
            dma((2, 4)),
            dma((2, 4)),
            dma((2, 4)),
            dma((2, 4, 4)),
            dma((2,)),
            dma((2,)),
            dma((4,)),
        ],
        compiler_params=pltpu.CompilerParams(
            collective_id=0, has_side_effects=True, vmem_limit_bytes=63 * 1024 * 1024
        ),
    )(act, gate_taps(gate_weight), cand_taps(cand_weight), bias)
    frames = out.reshape(2, ROWS, W, OWN).transpose(0, 1, 3, 2)
    return frames.reshape(2, ROWS, OWN * W)


def solution(mesh):
    placed = (
        P("space", "chan"),
        P(None, "space", "chan"),
        P("space", "chan"),
        P(None, "chan"),
        P("space", "chan"),
        P("chan"),
    )
    return jax.shard_map(
        local, mesh=mesh, in_specs=placed, out_specs=P(None, "space", "chan"), check_vma=False
    )
```

```python
import functools

import jax
import jax.numpy as jnp
from jax import lax
from jax.experimental import pallas as pl
from jax.experimental.pallas import tpu as pltpu
from jax.sharding import PartitionSpec as P

W = 96
ROWS = 3
CELLS = ROWS * W
HALO = (ROWS + 2) * W
OWN = 192
COND = 48
SHARD = 60
SLOT = 64
WIN = 256
BF = jnp.bfloat16
F32 = jnp.float32
PAIRS = tuple(
    (t, n)
    for t in range(1, 8)
    for n in range(8)
    if max(240 * t, 384 + 192 * n) < min(240 * t + 240, 576 + 192 * n)
)


def gate_taps(raw):
    taps = raw.reshape(SHARD, OWN, 2, 3, 3).transpose(3, 4, 0, 2, 1).reshape(9, SHARD, 2 * OWN)
    return jnp.pad(taps, ((0, 0), (0, SLOT - SHARD), (0, 0)))


def cand_taps(raw):
    taps = raw.reshape(30, OWN, 2, 9).transpose(3, 2, 0, 1)
    taps = jnp.pad(taps, ((0, 0), (0, 0), (0, 2), (0, 0)))
    return jnp.concatenate([taps[:, 0], taps[:, 1]], axis=2)


def kernel(
    act_ref, wg_ref, wc_ref, bias_ref, out_ref,
    init, gbuf0, sbuf, gbuf1, wg, wc, xs, emat, acc, cacc, upd, prev,
    fresh, landed, sib_bias,
    xsend, xrecv, wsend, wz, wl, wr, wo, wd, osem, orecv, bsem,
):
    s = lax.axis_index("space")
    ch = lax.axis_index("chan")
    x, z = s // 8, s % 8
    b, y, c = z % 2, ch // 2, ch % 2
    job_row = s - b + c
    job_chan = 2 * y + b
    right = (x + 1) % 4
    left = (x + 3) % 4
    opposite = (x + 2) % 4

    barrier = pltpu.get_barrier_semaphore()

    def greet(space, chan):
        pl.semaphore_signal(
            barrier, inc=1, device_id=(space, chan), device_id_type=pl.DeviceIdType.MESH
        )

    def greet_line(i, carry):
        space, chan = 8 * x + i // 2, 2 * y + i % 2

        @pl.when(jnp.logical_or(space != s, chan != ch))
        def _():
            greet(space, chan)

        return carry

    lax.fori_loop(0, 16, greet_line, 0)
    greet(8 * right + z, ch)
    greet(8 * left + z, ch)
    up = 2 * ((y + 1) % 4) + c
    down = 2 * ((y + 3) % 4) + c
    greet(s, up)
    greet(s, down)
    first = jnp.logical_and(z < 2, c == 0)
    last = jnp.logical_and(z >= 6, c == 1)

    @pl.when(first)
    def _():
        greet(8 * left + 6 + b, 2 * y + 1)

    @pl.when(last)
    def _():
        greet(8 * right + b, 2 * y)

    pl.semaphore_wait(barrier, 19 + jnp.logical_or(first, last).astype(jnp.int32))

    def remote(src, dst, send, recv, space, chan):
        return pltpu.make_async_remote_copy(
            src_ref=src, dst_ref=dst, send_sem=send, recv_sem=recv,
            device_id=(space, chan), device_id_type=pl.DeviceIdType.MESH,
        )

    def push(src, dst, send, recv, space, chan):
        mine = jnp.logical_and(space == s, chan == ch)

        @pl.when(mine)
        def _():
            pltpu.make_async_copy(src, dst, recv).start()

        @pl.when(jnp.logical_not(mine))
        def _():
            remote(src, dst, send, recv, space, chan).start()

    def sent(src, dst, send, recv, space, chan):
        mine = jnp.logical_and(space == s, chan == ch)

        @pl.when(jnp.logical_not(mine))
        def _():
            remote(src, dst, send, recv, space, chan).wait_send()

    def arrived(dst, recv):
        pltpu.make_async_copy(dst, dst, recv).wait()

    mate = s + 1 - 2 * b
    spans = {
        HALO: ((W, CELLS // 2), (W + CELLS // 2, CELLS // 2), (0, W), (4 * W, W)),
        HALO // 2: ((48, 80), (128, 64), (0, 48), (192, 48)),
    }
    blocks = [2 * ((y + d) % 4) + b for d in (0, 3, 1, 2)]
    twins = [2 * ((y + d) % 4) + 1 - b for d in (0, 3, 1, 2)]

    def edge(k, buf, down_edge):
        n = job_chan
        to_row = (job_row + (1 if down_edge else 31)) % 32
        unit = buf.shape[1] // 5
        src = buf.at[n, pl.ds(3 * unit if down_edge else unit, unit)]
        dst = buf.at[n, pl.ds(0 if down_edge else 4 * unit, unit)]
        i = 0 if down_edge else 1
        return remote(src, dst, xsend.at[i], xrecv.at[k, 32 + i],
                      to_row - to_row % 2 + b, 2 * y + to_row % 2)

    def part(buf, which, n):
        return buf.at[n, pl.ds(*spans[buf.shape[1]][which])]

    def move(k, buf, which, n, i, space, chan):
        ref = part(buf, which, n)
        send = xsend.at[2 + 14 * (which // 2) + i]
        return remote(ref, ref, send, xrecv.at[k, 8 * which + n], space, chan)

    def moves(k, buf, g):
        p, q = 2 * g, 2 * g + 1
        own_a = [move(k, buf, p, blocks[0], 0, s, up), move(k, buf, p, blocks[0], 1, s, down)]
        own_b = [move(k, buf, q, blocks[0], 2, mate, ch),
                 move(k, buf, q, blocks[0], 3, s, up), move(k, buf, q, blocks[0], 4, s, down)]
        on_a = [move(k, buf, p, blocks[d], 5 + d, mate, ch) for d in range(4)]
        pass_a = move(k, buf, p, blocks[1], 9, s, up)
        mate_b = [move(k, buf, q, twins[0], 10, s, up), move(k, buf, q, twins[0], 11, s, down)]
        pass_b = [move(k, buf, q, blocks[2], 12, s, down), move(k, buf, q, twins[2], 13, s, down)]
        return own_a, own_b, on_a, pass_a, mate_b, pass_b

    def got(k, buf, which, n):
        arrived(part(buf, which, n), xrecv.at[k, 8 * which + n])

    def edges_out(k, buf):
        edge(k, buf, True).start()
        edge(k, buf, False).start()

    def exchange_own(k, buf, g):
        own_a, own_b, on_a, _, _, _ = moves(k, buf, g)
        if g == 1:
            arrived(part(buf, 2, job_chan), xrecv.at[k, 32])
            arrived(part(buf, 3, job_chan), xrecv.at[k, 33])
        for m in [own_b[0]] + own_a + [on_a[0]] + own_b[1:]:
            m.start()

    def exchange_on(k, buf, g):
        _, _, on_a, pass_a, mate_b, pass_b = moves(k, buf, g)
        p, q = 2 * g, 2 * g + 1
        got(k, buf, q, twins[0])
        for m in mate_b:
            m.start()
        got(k, buf, p, blocks[1])
        pass_a.start()
        on_a[1].start()
        got(k, buf, p, blocks[2])
        on_a[2].start()
        got(k, buf, q, blocks[2])
        pass_b[0].start()
        got(k, buf, q, twins[2])
        pass_b[1].start()

    def exchange(k, buf):
        exchange_own(k, buf, 0)
        exchange_own(k, buf, 1)
        exchange_rest(k, buf)

    def exchange_rest(k, buf, between=lambda: None):
        exchange_on(k, buf, 0)
        between()
        exchange_on(k, buf, 1)
        for g in range(2):
            got(k, buf, 2 * g, blocks[3])
            moves(k, buf, g)[2][3].start()

    def exchanged(k, buf):
        for g in range(2):
            for d in range(4):
                got(k, buf, 2 * g, twins[d])
            for d in (1, 3):
                got(k, buf, 2 * g + 1, blocks[d])
                got(k, buf, 2 * g + 1, twins[d])

    def exchange_sent(k, buf):
        edge(k, buf, True).wait_send()
        edge(k, buf, False).wait_send()
        for g in range(2):
            own_a, own_b, on_a, pass_a, mate_b, pass_b = moves(k, buf, g)
            for m in own_a + own_b + on_a + [pass_a] + mate_b + pass_b:
                m.wait_send()

    def own_rows(buf):
        return buf.at[job_chan, pl.ds(W, CELLS)]

    group = z // 4
    spot = z % 4
    mine = ((wg_ref, wg), (wc_ref, wc))

    def kernel_z(kind, act, i):
        src, buf = mine[kind]
        to = (z // 2 + (0 if i == 0 else jnp.where(c == 0, i, 4 - i))) % 4
        act(src, buf.at[2 * x + group, :, spot], wsend.at[kind, i], wz.at[kind, spot],
            8 * x + 2 * to + c, 2 * y + group)

    lag = (z // 2 + 8 - 2 * c) % 4
    head = jnp.where(b == 0, jnp.where(lag == 0, 0, 2), jnp.where(lag == 1, 2, 0))
    turn = [(i + head) % 4 for i in range(4)]

    here, lower, upper, across = 2 * x + c, 2 * left + c, 2 * right + c, 2 * opposite + c

    def hop(kind, t, i, send, recv, space, chan):
        buf = mine[kind][1]
        return remote(buf.at[t, :, i], buf.at[t, :, i], wsend.at[kind, send], recv, space, chan)

    def go_right(kind, i):
        return hop(kind, here, i, 4 + i, wl.at[kind, i], 8 * right + z, ch)

    def go_left(kind, i):
        return hop(kind, here, i, 8 + i, wr.at[kind, i], 8 * left + z, ch)

    def pass_right(kind, i):
        return hop(kind, lower, i, 12 + i, wo.at[kind, i], 8 * right + z, ch)

    def pass_left(kind, i):
        return hop(kind, upper, i, 12 + i, wo.at[kind, i], 8 * left + z, ch)

    def share(kind, j, i):
        t = (here, lower, upper, across)[j]
        return hop(kind, t, i, 16 + 4 * j + i, wd.at[kind, j, i], s, 2 * y + 1 - c)

    def piece(kind, t, i):
        return mine[kind][1].at[t, :, i]

    def onward(kind, parity, i):
        return hop(kind, here, i, 2 if parity == 0 else 32, wz.at[kind, i],
                   8 * x + (z + jnp.where(b == 0, 2, 6)) % 8, ch)

    def passes_on(i):
        source = 2 * c + i // 2
        steps = jnp.where(b == 0, z // 2 - source + 4, source - z // 2 + 4) % 4
        return steps == 1

    def kernel_relay(kind):
        for parity, i in zip((0, 1, 0, 1), turn):
            @pl.when(passes_on(i))
            def _():
                arrived(piece(kind, here, i), wz.at[kind, i])
                onward(kind, parity, i).start()

    def kernel_own(kind, relayed, pair):
        for parity, i in zip((0, 1), turn[2 * pair:2 * pair + 2]):
            if relayed:
                @pl.when(jnp.logical_not(passes_on(i)))
                def _():
                    arrived(piece(kind, here, i), wz.at[kind, i])
            else:
                arrived(piece(kind, here, i), wz.at[kind, i])

                @pl.when(passes_on(i))
                def _():
                    onward(kind, parity, i).start()
            go_right(kind, i).start()
            go_left(kind, i).start()
            share(kind, 0, i).start()

    def kernel_sides(kind, pair):
        for parity, i in zip((0, 1), turn[2 * pair:2 * pair + 2]):
            arrived(piece(kind, lower, i), wl.at[kind, i])
            if parity == 0:
                pass_right(kind, i).start()
            share(kind, 1, i).start()
            arrived(piece(kind, upper, i), wr.at[kind, i])
            if parity == 1:
                pass_left(kind, i).start()
            share(kind, 2, i).start()

    def kernel_across(kind):
        for parity, i in zip((0, 1, 0, 1), turn):
            arrived(piece(kind, across, i), wo.at[kind, i])
            share(kind, 3, i).start()

    def kernel_shared(kind, j):
        t = 2 * ((here, lower, upper, across)[j] // 2) + 1 - c
        for i in range(4):
            arrived(piece(kind, t, i), wd.at[kind, j, i])
        return t

    def kernel_sent(kind):
        for i in (0, 3) if kind == 0 else (0, 1, 3):
            kernel_z(kind, sent, i)
        for parity, i in zip((0, 1, 0, 1), turn):
            @pl.when(passes_on(i))
            def _():
                onward(kind, parity, i).wait_send()
        for i in range(4):
            go_right(kind, i).wait_send()
            go_left(kind, i).wait_send()
            if i % 2 == 0:
                pass_right(kind, i).wait_send()
            else:
                pass_left(kind, i).wait_send()
            for j in range(4):
                share(kind, j, i).wait_send()

    def slot_channel(order, t, rows):
        j = lax.broadcasted_iota(jnp.int32, (rows, WIN), 1)
        if order == 0:
            r = j % SLOT
            return jnp.where(r < SHARD, SHARD * (4 * t + j // SLOT) + r, -1)
        m = j % 32
        return jnp.where(m < 30, SHARD * (4 * t + j % 128 // 32) + 2 * m + j // 128, -1)

    def spread(order, t, v):
        cell = lax.broadcasted_iota(jnp.int32, (HALO, WIN), 0)
        col = cell % W
        inside = jnp.logical_and(
            jnp.logical_or(cell >= W, job_row > 0),
            jnp.logical_or(cell < 4 * W, job_row < 31),
        )
        v = jnp.where(inside, v, 0.0)
        low = jnp.where(col == 0, 0.0, pltpu.roll(v, 1, 0))
        high = jnp.where(col == W - 1, 0.0, pltpu.roll(v, HALO - 1, 0))
        for d, shifted in enumerate((low, v, high)):
            shifted = shifted.astype(BF)
            if order == 0:
                xs[:, 768 * t + 256 * d:768 * t + 256 * d + 256] = shifted
            else:
                for p in range(2):
                    at = 768 * t + 384 * p + 128 * d
                    xs[:, at:at + 128] = shifted[:, 128 * p:128 * p + 128]

    def cond_slots(step, order, t):
        v = jnp.zeros((HALO, WIN), F32)
        lane = lax.broadcasted_iota(jnp.int32, (128, WIN), 0)
        want = slot_channel(order, t, 128)
        for n in range(5 * t, min(8, 5 * t + 5)):
            here_n = jnp.logical_and(lane >= COND * step, lane < COND * step + COND)
            hit = jnp.logical_and(here_n, want == COND * n + lane - COND * step)
            e = hit.astype(F32).astype(BF)
            v = v + jnp.dot(init[n, :, 0:128], e, preferred_element_type=F32)
        return v

    def build(step, order, buf, base):
        for t in range(1, 8):
            v = cond_slots(step, order, 1) if t == 1 else jnp.zeros((HALO, WIN), F32)
            for q, (pt, n) in enumerate(PAIRS):
                if pt == t:
                    e = emat[order, q]
                    low = jnp.dot(buf[n, :, base:base + OWN], e[64:], preferred_element_type=F32)
                    if buf.shape[1] < HALO:
                        high = jnp.dot(buf[n, :, 128:384], e, preferred_element_type=F32)
                        low = jnp.concatenate(
                            [low.reshape(5, 48, WIN), high.reshape(5, 48, WIN)], axis=1
                        ).reshape(HALO, WIN)
                    v = v + low
            spread(order, t, v)

    def window(buf, total, t):
        depth = 2 * OWN if total is cacc else 768
        for p in range(768 // depth):
            lane = pl.multiple_of(768 * t + depth * p, depth)
            sums = total.at[p] if total is cacc else total
            for a in range(3):
                sums[...] += jnp.dot(
                    xs[pl.ds(a * W, CELLS), pl.ds(lane, depth)],
                    buf[t, 3 * a:3 * a + 3].reshape(depth, 2 * OWN),
                    preferred_element_type=F32,
                )

    def bias(row):
        return jnp.where(b == c, bias_ref[row:row + 1, 0:OWN], sib_bias[row:row + 1, 0:OWN])

    def pack(v, buf):
        acc[:, 0:OWN] = v
        flat = acc[...]
        moved = pltpu.roll(flat, OWN, 1)
        lane = lax.broadcasted_iota(jnp.int32, (48, 2 * OWN), 1)
        for r in range(ROWS):
            both = jnp.where(lane < OWN, flat[W * r:W * r + 48], moved[W * r + 48:W * r + W])
            buf[job_chan, pl.ds(48 + 48 * r, 48), :] = both.astype(BF)

    def finish_gate(buf):
        pre = acc[...]
        upd[...] = jax.nn.sigmoid(pre[:, :OWN] + bias(0))
        reset = jax.nn.sigmoid(pltpu.roll(pre, OWN, 1)[:, :OWN] + bias(1))
        pack(reset * prev[...], buf)

    def finish_cand(k):
        candidate = jnp.tanh(cacc[0][:, :OWN] + pltpu.roll(cacc[1], OWN, 1)[:, :OWN] + bias(2))
        u = upd[...]
        new = ((1.0 - u) * prev[...] + u * candidate).astype(BF)
        fresh[k] = new
        prev[...] = new.astype(F32)

    def deliver(k, act):
        act(fresh.at[k], landed.at[k], osem.at[k], orecv.at[k], job_row, job_chan)

    def kernel_z_rest():
        kernel_z(0, sent, 1)
        kernel_z(0, push, 3)

    kernel_z(0, push, 0)
    kernel_z(0, push, 1)
    first_copy = (act_ref, init.at[ch, pl.ds(W, CELLS)], bsem.at[2], bsem.at[3], job_row, job_chan)
    push(*first_copy)
    bias_copy = remote(bias_ref, sib_bias, bsem.at[0], bsem.at[1], s, 2 * y + 1 - c)
    bias_copy.start()
    late = jnp.where(b == 0, lag, (4 - lag) % 4) == jnp.where(b == 0, 3, 2)
    pl.when(late)(kernel_z_rest)
    kernel_own(0, False, 0)
    pl.when(jnp.logical_not(late))(kernel_z_rest)
    arrived(own_rows(init), bsem.at[3])
    edges_out(0, init)
    kernel_own(0, False, 1)
    for i in (0, 1, 3):
        kernel_z(1, push, i)
    exchange_own(0, init, 0)
    exchange_own(0, init, 1)
    kernel_sides(0, 0)
    for order in range(2):
        for q, (t, n) in enumerate(PAIRS):
            lane = lax.broadcasted_iota(jnp.int32, (256, WIN), 0)
            hit = slot_channel(order, t, 256) == 320 + 192 * n + lane
            hit = jnp.logical_and(hit, lane >= 64)
            emat[order, q] = hit.astype(F32).astype(BF)
    acc[...] = jnp.zeros_like(acc)
    cacc[...] = jnp.zeros_like(cacc)
    exchange_rest(0, init)
    kernel_relay(1)
    kernel_sides(0, 1)
    kernel_own(1, True, 0)
    kernel_own(1, True, 1)
    sent(*first_copy)
    bias_copy.wait()
    exchanged(0, init)
    prev[...] = init[job_chan, pl.ds(W, CELLS), 128:128 + OWN].astype(F32)
    spread(0, 0, cond_slots(0, 0, 0))
    build(0, 0, init, 128)

    def shared_window(kind, buf, total, j):
        window(buf, total, kernel_shared(kind, j))

    window(wg, acc, here)
    window(wg, acc, lower)
    window(wg, acc, upper)
    shared_window(0, wg, acc, 0)
    shared_window(0, wg, acc, 1)
    shared_window(0, wg, acc, 2)
    kernel_across(0)
    window(wg, acc, across)
    shared_window(0, wg, acc, 3)
    exchange_sent(0, init)
    finish_gate(gbuf0)
    edges_out(1, gbuf0)
    exchange_own(1, gbuf0, 0)
    exchange_own(1, gbuf0, 1)
    kernel_sides(1, 0)
    exchange_rest(1, gbuf0, lambda: kernel_sides(1, 1))
    spread(1, 0, cond_slots(0, 1, 0))
    exchanged(1, gbuf0)
    build(0, 1, gbuf0, 0)
    window(wc, cacc, here)
    window(wc, cacc, lower)
    window(wc, cacc, upper)
    shared_window(1, wc, cacc, 0)
    shared_window(1, wc, cacc, 1)
    shared_window(1, wc, cacc, 2)
    kernel_across(1)
    window(wc, cacc, across)
    shared_window(1, wc, cacc, 3)
    exchange_sent(1, gbuf0)
    finish_cand(0)

    pack(prev[...], sbuf)
    edges_out(2, sbuf)
    deliver(0, push)
    acc[...] = jnp.zeros_like(acc)
    cacc[...] = jnp.zeros_like(cacc)
    exchange(2, sbuf)
    spread(0, 0, cond_slots(1, 0, 0))
    window(wg, acc, 0)
    exchanged(2, sbuf)
    build(1, 0, sbuf, 0)

    def all_windows(buf, total):
        def one(t, carry):
            window(buf, total, t)
            return carry

        lax.fori_loop(1, 8, one, 0)

    all_windows(wg, acc)
    exchange_sent(2, sbuf)
    finish_gate(gbuf1)
    edges_out(3, gbuf1)
    exchange(3, gbuf1)
    spread(1, 0, cond_slots(1, 1, 0))
    window(wc, cacc, 0)
    kernel_sent(0)
    kernel_sent(1)
    exchanged(3, gbuf1)
    build(1, 1, gbuf1, 0)
    all_windows(wc, cacc)
    exchange_sent(3, gbuf1)
    finish_cand(1)
    deliver(1, push)
    for k in range(2):
        arrived(landed.at[k], orecv.at[k])
        out_ref[k] = landed[k]
        deliver(k, sent)


def local(hidden, conditioning, gate_weight, gate_bias, cand_weight, cand_bias):
    state = hidden.reshape(ROWS, OWN, W).transpose(0, 2, 1).reshape(CELLS, OWN)
    cond = conditioning.reshape(2, ROWS, COND, W).transpose(1, 3, 0, 2).reshape(CELLS, 2 * COND)
    act = jnp.concatenate(
        [cond, jnp.zeros((CELLS, 32), BF), state, jnp.zeros((CELLS, 64), BF)], axis=1
    )
    bias = jnp.concatenate([gate_bias, cand_bias[None]], axis=0)
    bias = jnp.pad(bias, ((0, 5), (0, 64)))
    vmem = pl.BlockSpec(memory_space=pltpu.VMEM)
    dma = pltpu.SemaphoreType.DMA
    out = pl.pallas_call(
        kernel,
        out_shape=jax.ShapeDtypeStruct((2, CELLS, OWN), BF),
        in_specs=[vmem] * 4,
        out_specs=vmem,
        scratch_shapes=[
            pltpu.VMEM((8, HALO, 384), BF),
            pltpu.VMEM((8, HALO // 2, 2 * OWN), BF),
            pltpu.VMEM((8, HALO // 2, 2 * OWN), BF),
            pltpu.VMEM((8, HALO // 2, 2 * OWN), BF),
            pltpu.VMEM((8, 9, 4, SLOT, 2 * OWN), BF),
            pltpu.VMEM((8, 9, 4, SLOT // 2, 2 * OWN), BF),
            pltpu.VMEM((HALO, 8 * 768), BF),
            pltpu.VMEM((2, len(PAIRS), 256, WIN), BF),
            pltpu.VMEM((CELLS, 2 * OWN), F32),
            pltpu.VMEM((2, CELLS, 2 * OWN), F32),
            pltpu.VMEM((CELLS, OWN), F32),
            pltpu.VMEM((CELLS, OWN), F32),
            pltpu.VMEM((2, CELLS, OWN), BF),
            pltpu.VMEM((2, CELLS, OWN), BF),
            pltpu.VMEM((8, 256), F32),
            dma((30,)),
            dma((4, 34)),
            dma((2, 33)),
            dma((2, 4)),
            dma((2, 4)),
            dma((2, 4)),
            dma((2, 4)),
            dma((2, 4, 4)),
            dma((2,)),
            dma((2,)),
            dma((4,)),
        ],
        compiler_params=pltpu.CompilerParams(
            collective_id=0, has_side_effects=True, vmem_limit_bytes=63 * 1024 * 1024
        ),
    )(act, gate_taps(gate_weight), cand_taps(cand_weight), bias)
    frames = out.reshape(2, ROWS, W, OWN).transpose(0, 1, 3, 2)
    return frames.reshape(2, ROWS, OWN * W)


def solution(mesh):
    placed = (
        P("space", "chan"),
        P(None, "space", "chan"),
        P("space", "chan"),
        P(None, "chan"),
        P("space", "chan"),
        P("chan"),
    )
    return jax.shard_map(
        local, mesh=mesh, in_specs=placed, out_specs=P(None, "space", "chan"), check_vma=False
    )
```

```python
import functools

import jax
import jax.numpy as jnp
from jax import lax
from jax.experimental import pallas as pl
from jax.experimental.pallas import tpu as pltpu
from jax.sharding import PartitionSpec as P

W = 96
ROWS = 3
CELLS = ROWS * W
HALO = (ROWS + 2) * W
OWN = 192
COND = 48
SHARD = 60
SLOT = 64
WIN = 256
BF = jnp.bfloat16
F32 = jnp.float32
PAIRS = tuple(
    (t, n)
    for t in range(1, 8)
    for n in range(8)
    if max(240 * t, 384 + 192 * n) < min(240 * t + 240, 576 + 192 * n)
)


def gate_taps(raw):
    taps = raw.reshape(SHARD, OWN, 2, 3, 3).transpose(3, 4, 0, 2, 1).reshape(9, SHARD, 2 * OWN)
    return jnp.pad(taps, ((0, 0), (0, SLOT - SHARD), (0, 0)))


def cand_taps(raw):
    taps = raw.reshape(30, OWN, 2, 9).transpose(3, 2, 0, 1)
    taps = jnp.pad(taps, ((0, 0), (0, 0), (0, 2), (0, 0)))
    return jnp.concatenate([taps[:, 0], taps[:, 1]], axis=2)


def kernel(
    act_ref, wg_ref, wc_ref, bias_ref, out_ref,
    init, gbuf0, sbuf, gbuf1, wg, wc, xs, emat, acc, cacc, upd, prev,
    fresh, landed, sib_bias,
    xsend, xrecv, wsend, wz, wl, wr, wo, wd, osem, orecv, bsem,
):
    s = lax.axis_index("space")
    ch = lax.axis_index("chan")
    x, z = s // 8, s % 8
    b, y, c = z % 2, ch // 2, ch % 2
    job_row = s - b + c
    job_chan = 2 * y + b
    right = (x + 1) % 4
    left = (x + 3) % 4
    opposite = (x + 2) % 4

    barrier = pltpu.get_barrier_semaphore()

    def greet(space, chan):
        pl.semaphore_signal(
            barrier, inc=1, device_id=(space, chan), device_id_type=pl.DeviceIdType.MESH
        )

    def greet_line(i, carry):
        space, chan = 8 * x + i // 2, 2 * y + i % 2

        @pl.when(jnp.logical_or(space != s, chan != ch))
        def _():
            greet(space, chan)

        return carry

    lax.fori_loop(0, 16, greet_line, 0)
    greet(8 * right + z, ch)
    greet(8 * left + z, ch)
    up = 2 * ((y + 1) % 4) + c
    down = 2 * ((y + 3) % 4) + c
    greet(s, up)
    greet(s, down)
    first = jnp.logical_and(z < 2, c == 0)
    last = jnp.logical_and(z >= 6, c == 1)

    @pl.when(first)
    def _():
        greet(8 * left + 6 + b, 2 * y + 1)

    @pl.when(last)
    def _():
        greet(8 * right + b, 2 * y)

    pl.semaphore_wait(barrier, 19 + jnp.logical_or(first, last).astype(jnp.int32))

    def remote(src, dst, send, recv, space, chan):
        return pltpu.make_async_remote_copy(
            src_ref=src, dst_ref=dst, send_sem=send, recv_sem=recv,
            device_id=(space, chan), device_id_type=pl.DeviceIdType.MESH,
        )

    def push(src, dst, send, recv, space, chan):
        mine = jnp.logical_and(space == s, chan == ch)

        @pl.when(mine)
        def _():
            pltpu.make_async_copy(src, dst, recv).start()

        @pl.when(jnp.logical_not(mine))
        def _():
            remote(src, dst, send, recv, space, chan).start()

    def sent(src, dst, send, recv, space, chan):
        mine = jnp.logical_and(space == s, chan == ch)

        @pl.when(jnp.logical_not(mine))
        def _():
            remote(src, dst, send, recv, space, chan).wait_send()

    def arrived(dst, recv):
        pltpu.make_async_copy(dst, dst, recv).wait()

    mate = s + 1 - 2 * b
    spans = {
        HALO: ((W, CELLS // 2), (W + CELLS // 2, CELLS // 2), (0, W), (4 * W, W)),
        HALO // 2: ((48, 80), (128, 64), (0, 48), (192, 48)),
    }
    blocks = [2 * ((y + d) % 4) + b for d in (0, 3, 1, 2)]
    twins = [2 * ((y + d) % 4) + 1 - b for d in (0, 3, 1, 2)]

    def edge(k, buf, down_edge):
        n = job_chan
        to_row = (job_row + (1 if down_edge else 31)) % 32
        unit = buf.shape[1] // 5
        src = buf.at[n, pl.ds(3 * unit if down_edge else unit, unit)]
        dst = buf.at[n, pl.ds(0 if down_edge else 4 * unit, unit)]
        i = 0 if down_edge else 1
        return remote(src, dst, xsend.at[i], xrecv.at[k, 32 + i],
                      to_row - to_row % 2 + b, 2 * y + to_row % 2)

    def part(buf, which, n):
        return buf.at[n, pl.ds(*spans[buf.shape[1]][which])]

    def move(k, buf, which, n, i, space, chan):
        ref = part(buf, which, n)
        send = xsend.at[2 + 14 * (which // 2) + i]
        return remote(ref, ref, send, xrecv.at[k, 8 * which + n], space, chan)

    def moves(k, buf, g):
        p, q = 2 * g, 2 * g + 1
        own_a = [move(k, buf, p, blocks[0], 0, s, up), move(k, buf, p, blocks[0], 1, s, down)]
        own_b = [move(k, buf, q, blocks[0], 2, mate, ch),
                 move(k, buf, q, blocks[0], 3, s, up), move(k, buf, q, blocks[0], 4, s, down)]
        on_a = [move(k, buf, p, blocks[d], 5 + d, mate, ch) for d in range(4)]
        pass_a = move(k, buf, p, blocks[1], 9, s, up)
        mate_b = [move(k, buf, q, twins[0], 10, s, up), move(k, buf, q, twins[0], 11, s, down)]
        pass_b = [move(k, buf, q, blocks[2], 12, s, down), move(k, buf, q, twins[2], 13, s, down)]
        return own_a, own_b, on_a, pass_a, mate_b, pass_b

    def got(k, buf, which, n):
        arrived(part(buf, which, n), xrecv.at[k, 8 * which + n])

    def edges_out(k, buf):
        edge(k, buf, True).start()
        edge(k, buf, False).start()

    def exchange_own(k, buf, g):
        own_a, own_b, on_a, _, _, _ = moves(k, buf, g)
        if g == 1:
            arrived(part(buf, 2, job_chan), xrecv.at[k, 32])
            arrived(part(buf, 3, job_chan), xrecv.at[k, 33])
        for m in [own_b[0]] + own_a + [on_a[0]] + own_b[1:]:
            m.start()

    def exchange_on(k, buf, g):
        _, _, on_a, pass_a, mate_b, pass_b = moves(k, buf, g)
        p, q = 2 * g, 2 * g + 1
        got(k, buf, q, twins[0])
        for m in mate_b:
            m.start()
        got(k, buf, p, blocks[1])
        pass_a.start()
        on_a[1].start()
        got(k, buf, p, blocks[2])
        on_a[2].start()
        got(k, buf, q, blocks[2])
        pass_b[0].start()
        got(k, buf, q, twins[2])
        pass_b[1].start()

    def exchange(k, buf):
        exchange_own(k, buf, 0)
        exchange_own(k, buf, 1)
        exchange_rest(k, buf)

    def exchange_rest(k, buf, between=lambda: None):
        exchange_on(k, buf, 0)
        between()
        exchange_on(k, buf, 1)
        for g in range(2):
            got(k, buf, 2 * g, blocks[3])
            moves(k, buf, g)[2][3].start()

    def exchanged(k, buf):
        for g in range(2):
            for d in range(4):
                got(k, buf, 2 * g, twins[d])
            for d in (1, 3):
                got(k, buf, 2 * g + 1, blocks[d])
                got(k, buf, 2 * g + 1, twins[d])

    def exchange_sent(k, buf):
        edge(k, buf, True).wait_send()
        edge(k, buf, False).wait_send()
        for g in range(2):
            own_a, own_b, on_a, pass_a, mate_b, pass_b = moves(k, buf, g)
            for m in own_a + own_b + on_a + [pass_a] + mate_b + pass_b:
                m.wait_send()

    def own_rows(buf):
        return buf.at[job_chan, pl.ds(W, CELLS)]

    group = z // 4
    spot = z % 4
    mine = ((wg_ref, wg), (wc_ref, wc))

    def kernel_z(kind, act, i):
        src, buf = mine[kind]
        to = (z // 2 + (0 if i == 0 else jnp.where(c == 0, i, 4 - i))) % 4
        act(src, buf.at[2 * x + group, :, spot], wsend.at[kind, i], wz.at[kind, spot],
            8 * x + 2 * to + c, 2 * y + group)

    lag = (z // 2 + 8 - 2 * c) % 4
    head = jnp.where(b == 0, jnp.where(lag == 0, 0, 2), jnp.where(lag == 1, 2, 0))
    turn = [(i + head) % 4 for i in range(4)]

    here, lower, upper, across = 2 * x + c, 2 * left + c, 2 * right + c, 2 * opposite + c

    def hop(kind, t, i, send, recv, space, chan):
        buf = mine[kind][1]
        return remote(buf.at[t, :, i], buf.at[t, :, i], wsend.at[kind, send], recv, space, chan)

    def go_right(kind, i):
        return hop(kind, here, i, 4 + i, wl.at[kind, i], 8 * right + z, ch)

    def go_left(kind, i):
        return hop(kind, here, i, 8 + i, wr.at[kind, i], 8 * left + z, ch)

    def pass_right(kind, i):
        return hop(kind, lower, i, 12 + i, wo.at[kind, i], 8 * right + z, ch)

    def pass_left(kind, i):
        return hop(kind, upper, i, 12 + i, wo.at[kind, i], 8 * left + z, ch)

    def share(kind, j, i):
        t = (here, lower, upper, across)[j]
        return hop(kind, t, i, 16 + 4 * j + i, wd.at[kind, j, i], s, 2 * y + 1 - c)

    def piece(kind, t, i):
        return mine[kind][1].at[t, :, i]

    def onward(kind, parity, i):
        return hop(kind, here, i, 2 if parity == 0 else 32, wz.at[kind, i],
                   8 * x + (z + jnp.where(b == 0, 2, 6)) % 8, ch)

    def passes_on(i):
        source = 2 * c + i // 2
        steps = jnp.where(b == 0, z // 2 - source + 4, source - z // 2 + 4) % 4
        return steps == 1

    def kernel_relay(kind):
        for parity, i in zip((0, 1, 0, 1), turn):
            @pl.when(passes_on(i))
            def _():
                arrived(piece(kind, here, i), wz.at[kind, i])
                onward(kind, parity, i).start()

    def kernel_own(kind, relayed, pair):
        for parity, i in zip((0, 1), turn[2 * pair:2 * pair + 2]):
            if relayed:
                @pl.when(jnp.logical_not(passes_on(i)))
                def _():
                    arrived(piece(kind, here, i), wz.at[kind, i])
            else:
                arrived(piece(kind, here, i), wz.at[kind, i])

                @pl.when(passes_on(i))
                def _():
                    onward(kind, parity, i).start()
            go_right(kind, i).start()
            go_left(kind, i).start()
            share(kind, 0, i).start()

    def kernel_sides(kind, pair):
        for parity, i in zip((0, 1), turn[2 * pair:2 * pair + 2]):
            arrived(piece(kind, lower, i), wl.at[kind, i])
            if parity == 0:
                pass_right(kind, i).start()
            share(kind, 1, i).start()
            arrived(piece(kind, upper, i), wr.at[kind, i])
            if parity == 1:
                pass_left(kind, i).start()
            share(kind, 2, i).start()

    def kernel_across(kind):
        for parity, i in zip((0, 1, 0, 1), turn):
            arrived(piece(kind, across, i), wo.at[kind, i])
            share(kind, 3, i).start()

    def kernel_shared(kind, j):
        t = 2 * ((here, lower, upper, across)[j] // 2) + 1 - c
        for i in range(4):
            arrived(piece(kind, t, i), wd.at[kind, j, i])
        return t

    def kernel_sent(kind):
        for i in (0, 3) if kind == 0 else (0, 1, 3):
            kernel_z(kind, sent, i)
        for parity, i in zip((0, 1, 0, 1), turn):
            @pl.when(passes_on(i))
            def _():
                onward(kind, parity, i).wait_send()
        for i in range(4):
            go_right(kind, i).wait_send()
            go_left(kind, i).wait_send()
            if i % 2 == 0:
                pass_right(kind, i).wait_send()
            else:
                pass_left(kind, i).wait_send()
            for j in range(4):
                share(kind, j, i).wait_send()

    def slot_channel(order, t, rows):
        j = lax.broadcasted_iota(jnp.int32, (rows, WIN), 1)
        if order == 0:
            r = j % SLOT
            return jnp.where(r < SHARD, SHARD * (4 * t + j // SLOT) + r, -1)
        m = j % 32
        return jnp.where(m < 30, SHARD * (4 * t + j % 128 // 32) + 2 * m + j // 128, -1)

    def spread(order, t, v):
        cell = lax.broadcasted_iota(jnp.int32, (HALO, WIN), 0)
        col = cell % W
        inside = jnp.logical_and(
            jnp.logical_or(cell >= W, job_row > 0),
            jnp.logical_or(cell < 4 * W, job_row < 31),
        )
        v = jnp.where(inside, v, 0.0)
        low = jnp.where(col == 0, 0.0, pltpu.roll(v, 1, 0))
        high = jnp.where(col == W - 1, 0.0, pltpu.roll(v, HALO - 1, 0))
        for d, shifted in enumerate((low, v, high)):
            shifted = shifted.astype(BF)
            if order == 0:
                xs[:, 768 * t + 256 * d:768 * t + 256 * d + 256] = shifted
            else:
                for p in range(2):
                    at = 768 * t + 384 * p + 128 * d
                    xs[:, at:at + 128] = shifted[:, 128 * p:128 * p + 128]

    def cond_slots(step, order, t):
        v = jnp.zeros((HALO, WIN), F32)
        lane = lax.broadcasted_iota(jnp.int32, (128, WIN), 0)
        want = slot_channel(order, t, 128)
        for n in range(5 * t, min(8, 5 * t + 5)):
            here_n = jnp.logical_and(lane >= COND * step, lane < COND * step + COND)
            hit = jnp.logical_and(here_n, want == COND * n + lane - COND * step)
            e = hit.astype(F32).astype(BF)
            v = v + jnp.dot(init[n, :, 0:128], e, preferred_element_type=F32)
        return v

    def build(step, order, buf, base):
        for t in range(1, 8):
            v = cond_slots(step, order, 1) if t == 1 else jnp.zeros((HALO, WIN), F32)
            for q, (pt, n) in enumerate(PAIRS):
                if pt == t:
                    e = emat[order, q]
                    low = jnp.dot(buf[n, :, base:base + OWN], e[64:], preferred_element_type=F32)
                    if buf.shape[1] < HALO:
                        high = jnp.dot(buf[n, :, 128:384], e, preferred_element_type=F32)
                        low = jnp.concatenate(
                            [low.reshape(5, 48, WIN), high.reshape(5, 48, WIN)], axis=1
                        ).reshape(HALO, WIN)
                    v = v + low
            spread(order, t, v)

    def window(buf, total, t):
        depth = 2 * OWN if total is cacc else 768
        for p in range(768 // depth):
            lane = pl.multiple_of(768 * t + depth * p, depth)
            sums = total.at[p] if total is cacc else total
            for a in range(3):
                sums[...] += jnp.dot(
                    xs[pl.ds(a * W, CELLS), pl.ds(lane, depth)],
                    buf[t, 3 * a:3 * a + 3].reshape(depth, 2 * OWN),
                    preferred_element_type=F32,
                )

    def bias(row):
        return jnp.where(b == c, bias_ref[row:row + 1, 0:OWN], sib_bias[row:row + 1, 0:OWN])

    def pack(v, buf):
        acc[:, 0:OWN] = v
        flat = acc[...]
        moved = pltpu.roll(flat, OWN, 1)
        lane = lax.broadcasted_iota(jnp.int32, (48, 2 * OWN), 1)
        for r in range(ROWS):
            both = jnp.where(lane < OWN, flat[W * r:W * r + 48], moved[W * r + 48:W * r + W])
            buf[job_chan, pl.ds(48 + 48 * r, 48), :] = both.astype(BF)

    def finish_gate(buf):
        pre = acc[...]
        upd[...] = jax.nn.sigmoid(pre[:, :OWN] + bias(0))
        reset = jax.nn.sigmoid(pltpu.roll(pre, OWN, 1)[:, :OWN] + bias(1))
        pack(reset * prev[...], buf)

    def finish_cand(k):
        candidate = jnp.tanh(cacc[0][:, :OWN] + pltpu.roll(cacc[1], OWN, 1)[:, :OWN] + bias(2))
        u = upd[...]
        new = ((1.0 - u) * prev[...] + u * candidate).astype(BF)
        fresh[k] = new
        prev[...] = new.astype(F32)

    def deliver(k, act):
        act(fresh.at[k], landed.at[k], osem.at[k], orecv.at[k], job_row, job_chan)

    def kernel_z_rest():
        kernel_z(0, sent, 1)
        kernel_z(0, push, 3)

    kernel_z(0, push, 0)
    kernel_z(0, push, 1)
    first_copy = (act_ref, init.at[ch, pl.ds(W, CELLS)], bsem.at[2], bsem.at[3], job_row, job_chan)
    push(*first_copy)
    bias_copy = remote(bias_ref, sib_bias, bsem.at[0], bsem.at[1], s, 2 * y + 1 - c)
    bias_copy.start()
    late = jnp.where(b == 0, lag, (4 - lag) % 4) == jnp.where(b == 0, 3, 2)
    pl.when(late)(kernel_z_rest)
    kernel_own(0, False, 0)
    pl.when(jnp.logical_not(late))(kernel_z_rest)
    arrived(own_rows(init), bsem.at[3])
    edges_out(0, init)
    kernel_own(0, False, 1)
    for i in (0, 1, 3):
        kernel_z(1, push, i)
    exchange_own(0, init, 0)
    exchange_own(0, init, 1)
    kernel_sides(0, 0)
    for order in range(2):
        for q, (t, n) in enumerate(PAIRS):
            lane = lax.broadcasted_iota(jnp.int32, (256, WIN), 0)
            hit = slot_channel(order, t, 256) == 320 + 192 * n + lane
            hit = jnp.logical_and(hit, lane >= 64)
            emat[order, q] = hit.astype(F32).astype(BF)
    acc[...] = jnp.zeros_like(acc)
    cacc[...] = jnp.zeros_like(cacc)

    def more_kernel():
        kernel_sides(0, 1)
        kernel_relay(1)
        kernel_own(1, True, 0)
        kernel_own(1, True, 1)

    exchange_rest(0, init, more_kernel)
    sent(*first_copy)
    bias_copy.wait()
    exchanged(0, init)
    prev[...] = init[job_chan, pl.ds(W, CELLS), 128:128 + OWN].astype(F32)
    spread(0, 0, cond_slots(0, 0, 0))
    build(0, 0, init, 128)

    def shared_window(kind, buf, total, j):
        window(buf, total, kernel_shared(kind, j))

    window(wg, acc, here)
    window(wg, acc, lower)
    window(wg, acc, upper)
    shared_window(0, wg, acc, 0)
    shared_window(0, wg, acc, 1)
    shared_window(0, wg, acc, 2)
    kernel_across(0)
    window(wg, acc, across)
    shared_window(0, wg, acc, 3)
    exchange_sent(0, init)
    finish_gate(gbuf0)
    edges_out(1, gbuf0)
    exchange_own(1, gbuf0, 0)
    exchange_own(1, gbuf0, 1)
    kernel_sides(1, 0)
    exchange_rest(1, gbuf0, lambda: kernel_sides(1, 1))
    spread(1, 0, cond_slots(0, 1, 0))
    exchanged(1, gbuf0)
    build(0, 1, gbuf0, 0)
    window(wc, cacc, here)
    window(wc, cacc, lower)
    window(wc, cacc, upper)
    shared_window(1, wc, cacc, 0)
    shared_window(1, wc, cacc, 1)
    shared_window(1, wc, cacc, 2)
    kernel_across(1)
    window(wc, cacc, across)
    shared_window(1, wc, cacc, 3)
    exchange_sent(1, gbuf0)
    finish_cand(0)

    pack(prev[...], sbuf)
    edges_out(2, sbuf)
    deliver(0, push)
    acc[...] = jnp.zeros_like(acc)
    cacc[...] = jnp.zeros_like(cacc)
    exchange(2, sbuf)
    spread(0, 0, cond_slots(1, 0, 0))
    window(wg, acc, 0)
    exchanged(2, sbuf)
    build(1, 0, sbuf, 0)

    def all_windows(buf, total):
        def one(t, carry):
            window(buf, total, t)
            return carry

        lax.fori_loop(1, 8, one, 0)

    all_windows(wg, acc)
    exchange_sent(2, sbuf)
    finish_gate(gbuf1)
    edges_out(3, gbuf1)
    exchange(3, gbuf1)
    spread(1, 0, cond_slots(1, 1, 0))
    window(wc, cacc, 0)
    kernel_sent(0)
    kernel_sent(1)
    exchanged(3, gbuf1)
    build(1, 1, gbuf1, 0)
    all_windows(wc, cacc)
    exchange_sent(3, gbuf1)
    finish_cand(1)
    deliver(1, push)
    for k in range(2):
        arrived(landed.at[k], orecv.at[k])
        out_ref[k] = landed[k]
        deliver(k, sent)


def local(hidden, conditioning, gate_weight, gate_bias, cand_weight, cand_bias):
    state = hidden.reshape(ROWS, OWN, W).transpose(0, 2, 1).reshape(CELLS, OWN)
    cond = conditioning.reshape(2, ROWS, COND, W).transpose(1, 3, 0, 2).reshape(CELLS, 2 * COND)
    act = jnp.concatenate(
        [cond, jnp.zeros((CELLS, 32), BF), state, jnp.zeros((CELLS, 64), BF)], axis=1
    )
    bias = jnp.concatenate([gate_bias, cand_bias[None]], axis=0)
    bias = jnp.pad(bias, ((0, 5), (0, 64)))
    vmem = pl.BlockSpec(memory_space=pltpu.VMEM)
    dma = pltpu.SemaphoreType.DMA
    out = pl.pallas_call(
        kernel,
        out_shape=jax.ShapeDtypeStruct((2, CELLS, OWN), BF),
        in_specs=[vmem] * 4,
        out_specs=vmem,
        scratch_shapes=[
            pltpu.VMEM((8, HALO, 384), BF),
            pltpu.VMEM((8, HALO // 2, 2 * OWN), BF),
            pltpu.VMEM((8, HALO // 2, 2 * OWN), BF),
            pltpu.VMEM((8, HALO // 2, 2 * OWN), BF),
            pltpu.VMEM((8, 9, 4, SLOT, 2 * OWN), BF),
            pltpu.VMEM((8, 9, 4, SLOT // 2, 2 * OWN), BF),
            pltpu.VMEM((HALO, 8 * 768), BF),
            pltpu.VMEM((2, len(PAIRS), 256, WIN), BF),
            pltpu.VMEM((CELLS, 2 * OWN), F32),
            pltpu.VMEM((2, CELLS, 2 * OWN), F32),
            pltpu.VMEM((CELLS, OWN), F32),
            pltpu.VMEM((CELLS, OWN), F32),
            pltpu.VMEM((2, CELLS, OWN), BF),
            pltpu.VMEM((2, CELLS, OWN), BF),
            pltpu.VMEM((8, 256), F32),
            dma((30,)),
            dma((4, 34)),
            dma((2, 33)),
            dma((2, 4)),
            dma((2, 4)),
            dma((2, 4)),
            dma((2, 4)),
            dma((2, 4, 4)),
            dma((2,)),
            dma((2,)),
            dma((4,)),
        ],
        compiler_params=pltpu.CompilerParams(
            collective_id=0, has_side_effects=True, vmem_limit_bytes=63 * 1024 * 1024
        ),
    )(act, gate_taps(gate_weight), cand_taps(cand_weight), bias)
    frames = out.reshape(2, ROWS, W, OWN).transpose(0, 1, 3, 2)
    return frames.reshape(2, ROWS, OWN * W)


def solution(mesh):
    placed = (
        P("space", "chan"),
        P(None, "space", "chan"),
        P("space", "chan"),
        P(None, "chan"),
        P("space", "chan"),
        P("chan"),
    )
    return jax.shard_map(
        local, mesh=mesh, in_specs=placed, out_specs=P(None, "space", "chan"), check_vma=False
    )
```
